256 devices in a mesh: group: 8 (over y, core), ctx: 32 (over z, x).
Axes of the slice: x: 4, y: 4, z: 8, core: 2. Of those that a mesh axis runs over, the one named last changes fastest.
Arguments:
- query_raw: bfloat16 [8, 512, 4096], P('group', 'ctx'), may hold values from -6 to 6
- suffix_keyval: bfloat16 [8, 512, 1024], P('group', 'ctx'), may hold values from -12 to 12
- query_gain: float32 [128], replicated, may hold values from 0.5 to 1.5
- key_norm_gain: float32 [128], replicated, may hold values from 1.5 to 4
- positions: int32 [8, 512], P('group', 'ctx'), may hold values from 8192 to 25087, as said below
- prefix_length: int32 [8], P('group'), may hold values from 8192 to 24576
- page_owner: int32 [8, 1536, 1], P('group', 'ctx'), may hold values from 0 to 7; in each aligned block of 48 rows (0 to 47, 48 to 95, ..., all dimensions but the last counted through in order) at most 12 rows name the same one
- page_slot: int32 [8, 1536], P('group', 'ctx'), may hold values from 0 to 95
- cache_pool: bfloat16 [8, 3072, 16, 1024], P('group', 'ctx'), may hold values from -22 to 22
Outputs:
- attention_out: bfloat16 [8, 512, 4096], P('group', 'ctx')
The draws below stay inside these ranges and needn't reach their ends.
Inputs may be any that keep to these rules, and one draw needn't show every extreme that they name: positions[g, i] = prefix_length[g] + i. `page_owner`: among the 48 pages of one device (aligned blocks of pages), at most 12 name the same owner group.
All inputs are finite; a program needn't handle non-finite values.
Results may differ from the reference program's by a relative error of at most 0.02.
Values may be sent and summed in bfloat16 or wider, within the bound.
A program may use at most 128 MiB of HBM per device.

```python
import math
import jax
import jax.numpy as jnp
import numpy as np
from jax import lax

QUERY_HEAD_COUNT = 32
KEYVALUE_HEADS = 4
HEAD_SIZE = 128
PAGE = 16
SUFFIX_TOKENS = 512
PAGES_DEV = 48
POOL_DEV = 96
CAP = 12
GROUPS = 8
PAGES = 1536
PREFIX_SLOTS = 24576
POOL_ALL = 3072
KEYVALUE_WIDTH = 1024
QW = 4096


def shared_lengths(key):
    inner_key = jax.random.fold_in(key, 101)
    length_key, pick_key = jax.random.split(inner_key)
    lengths = jax.random.randint(length_key, (GROUPS,), PREFIX_SLOTS // 3, PREFIX_SLOTS + 1)
    longest = jax.random.randint(pick_key, (), 0, GROUPS)
    return jnp.where(jnp.arange(GROUPS) == longest, PREFIX_SLOTS, lengths).astype(jnp.int32)


def draw_prefix_length(key, part):
    return shared_lengths(key)


def draw_positions(key, part):
    return (shared_lengths(key)[:, None] + jnp.arange(SUFFIX_TOKENS, dtype=jnp.int32)[None, :]).astype(jnp.int32)


def draw_query_raw(key, part):
    inner_key = jax.random.fold_in(key, 303)
    shape = (GROUPS, SUFFIX_TOKENS, QW)
    return jax.random.truncated_normal(inner_key, -6.0, 6.0, shape, jnp.float32).astype(jnp.bfloat16)


def draw_cache_pool(key, part):
    inner_key = jax.random.fold_in(key, 404)
    shape = (GROUPS, POOL_ALL, PAGE, KEYVALUE_WIDTH)
    key_column_block = jnp.arange(KEYVALUE_WIDTH) < KEYVALUE_HEADS * HEAD_SIZE
    return (jax.random.truncated_normal(inner_key, -6.0, 6.0, shape, jnp.float32) * jnp.where(key_column_block, 2.5, 2.0)).astype(jnp.bfloat16)


def plant(drawn, rng, low, largest):
    spot = [jax.random.randint(jax.random.fold_in(rng, axis), (), 0, length) for axis, length in enumerate(drawn.shape)]
    widest = drawn.shape.index(max(drawn.shape))
    neighbour = spot[:widest] + [(spot[widest] + 1) % drawn.shape[widest]] + spot[widest + 1:]
    return drawn.at[tuple(spot)].set(low).at[tuple(neighbour)].set(largest)


def shard_levels(own_key, dims, cuts, smallest, largest):
    def one(axis_at, parts):
        steps = jax.random.uniform(jax.random.fold_in(jax.random.fold_in(own_key, 6), axis_at), (parts,), jnp.float32, smallest / len(cuts), largest / len(cuts))
        return jnp.repeat(jnp.exp(steps), dims[axis_at] // parts).reshape((-1,) + (1,) * (len(dims) - axis_at - 1))

    level = one(*cuts[0])
    for cut in cuts[1:]:
        level = level * one(*cut)
    return level


def shared_out(key, own, number, rows, count, top, most, lean):
    ranking = jax.random.permutation(key, count)
    crowded, usual = shares(count, rows * top, most, lean, True), shares(count, rows * top, most, lean, False)
    places = jnp.arange(count)

    def named(sizes, offset_by):
        used = int((sizes > 0).sum())
        fixed = max(1, used // 4)
        passed = fixed + (places - fixed + offset_by * (used - fixed)) % max(1, count - fixed)
        return jnp.zeros((count,), jnp.int32).at[ranking[jnp.where(places < fixed, places, passed)]].set(jnp.asarray(sizes, jnp.int32))

    sizes = jnp.where(number % 4 == 0, named(crowded, number // 4), named(usual, number - number // 4 - 1))
    mixed = jax.random.permutation(jax.random.fold_in(own, 3), count)
    giver, sink = mixed[0:count // 2 * 2:2], mixed[1:count // 2 * 2:2]
    slack = jnp.minimum(sizes[giver] - 1, most - sizes[sink]) // 2
    slack = jnp.where((giver == ranking[0]) | (sink == ranking[0]) | (sizes[sink] == 0), 0, jnp.maximum(slack, 0))
    passed = jax.random.randint(jax.random.fold_in(own, 4), (count // 2,), 0, 1 << 20) % (slack + 1)
    sizes = sizes.at[giver].add(-passed).at[sink].add(passed)
    members = jnp.searchsorted(jnp.cumsum(sizes), jnp.arange(rows * top), side="right").astype(jnp.int32)
    table = members.reshape(top, rows).T
    table = table[jax.random.permutation(jax.random.fold_in(own, 1), rows)]
    offset_by = jax.random.randint(jax.random.fold_in(own, 2), (rows, 1), 0, top)
    return jnp.take_along_axis(table, (jnp.arange(top)[None, :] + offset_by) % top, axis=1)


def shares(count, total, reach, skew, full):
    portions = [(1 << 20) // math.isqrt(standing ** skew) + 1 for standing in range(1, count + 1)]
    largest = reach if full else min(reach, max(-(-total // count), total * portions[0] // sum(portions)))
    least = 1 if total - largest >= count - 1 else 0
    counts, spare = [largest] + [least] * (count - 1), total - largest - least * (count - 1)
    while spare > 0:
        movable = [i for i in range(1, count) if counts[i] < largest] or [i for i in range(1, count) if counts[i] < reach]
        mass, budget = sum([portions[i] for i in movable]), spare
        for i in movable:
            extra = min(reach - counts[i], max(1, budget * portions[i] // mass), spare)
            counts[i] = counts[i] + extra
            spare = spare - extra
    return np.array(counts)


def normal_values(own_key, dims, spread, bound, cuts=(), held_as=jnp.bfloat16):
    result = spread * jax.random.normal(own_key, dims, jnp.float32)
    if cuts:
        result = result * shard_levels(own_key, dims, cuts, -0.22, 0.18)
    return jnp.clip(result, -bound, bound).astype(held_as)


def setup_inputs(seed: int = 0) -> dict:
    streams_of = jax.random.split(jax.random.key(seed), 10)
    query_raw = draw_query_raw(jax.random.fold_in(streams_of[9], 71), 0)
    suffix_keyval = normal_values(streams_of[1], (GROUPS, SUFFIX_TOKENS, KEYVALUE_WIDTH), 2.0, 12.0, ((0, 8), (1, 32)))
    query_gain = jnp.clip(1.0 + 0.1 * jax.random.normal(streams_of[2], (HEAD_SIZE,), jnp.float32), 0.5, 1.5)
    key_norm_gain = jnp.clip(jnp.exp(jax.random.uniform(streams_of[3], (HEAD_SIZE,), jnp.float32, math.log(1.5), math.log(4.0))), 1.5, 4.0)
    positions = draw_positions(jax.random.fold_in(streams_of[9], 71), 0)
    prefix_length = draw_prefix_length(jax.random.fold_in(streams_of[9], 71), 0)
    page_owner_keys = jax.random.split(jax.random.fold_in(streams_of[6], 1), GROUPS * PAGES // PAGES_DEV)
    page_owner_turns = jax.random.permutation(jax.random.fold_in(streams_of[6], 3), GROUPS * PAGES // PAGES_DEV)
    page_owner = jax.vmap(lambda own, number: shared_out(jax.random.fold_in(streams_of[6], 2), own, number, PAGES_DEV, GROUPS, 1, CAP, 1))(page_owner_keys, page_owner_turns).reshape((GROUPS, PAGES, 1))
    page_slot = plant(jax.random.randint(streams_of[7], (GROUPS, PAGES), 0, POOL_DEV), jax.random.fold_in(streams_of[7], 1), 0, POOL_DEV - 1).astype(jnp.int32)
    cache_pool = draw_cache_pool(jax.random.fold_in(streams_of[9], 71), 0)
    return dict(query_raw=query_raw, suffix_keyval=suffix_keyval, query_gain=query_gain, key_norm_gain=key_norm_gain, positions=positions, prefix_length=prefix_length, page_owner=page_owner, page_slot=page_slot, cache_pool=cache_pool)


epsilon = 1e-06
floor_score = -1e+30

def apply_rotation(raw_rows, gain, token_places):
    head_width = raw_rows.shape[-1]
    half_width = head_width // 2
    scaled = raw_rows * lax.rsqrt(lax.optimization_barrier(jnp.mean(raw_rows * raw_rows, axis=-1, keepdims=True)) + epsilon) * gain
    frequency = 1000000.0 ** (-(2.0 / head_width) * jnp.arange(half_width, dtype=jnp.float32))
    angles = token_places.astype(jnp.float32)[:, None] * frequency[None, :]
    cosine = jnp.cos(angles)[:, None, :]
    sine_part = jnp.sin(angles)[:, None, :]
    lower_half = scaled[..., :half_width]
    upper_half = scaled[..., half_width:]
    return jnp.concatenate([lower_half * cosine - upper_half * sine_part, upper_half * cosine + lower_half * sine_part], axis=-1)

def reference(query_raw, suffix_keyval, query_gain, key_norm_gain, positions, prefix_length, page_owner, page_slot, cache_pool):
    query_group_ratio = QUERY_HEAD_COUNT // KEYVALUE_HEADS
    key_value_split = KEYVALUE_HEADS * HEAD_SIZE
    total_keys = PREFIX_SLOTS + SUFFIX_TOKENS

    def one_group(group_index):
        token_places = positions[group_index]
        query_rows = apply_rotation(query_raw[group_index].astype(jnp.float32).reshape(SUFFIX_TOKENS, QUERY_HEAD_COUNT, HEAD_SIZE), query_gain, token_places)
        query_rows = query_rows.astype(jnp.bfloat16)
        newest_rows = suffix_keyval[group_index]
        key_rotated = apply_rotation(newest_rows[:, :key_value_split].astype(jnp.float32).reshape(SUFFIX_TOKENS, KEYVALUE_HEADS, HEAD_SIZE), key_norm_gain, token_places)
        key_rotated = key_rotated.astype(jnp.bfloat16)
        suffix_value = newest_rows[:, key_value_split:].reshape(SUFFIX_TOKENS, KEYVALUE_HEADS, HEAD_SIZE)
        owner_ids = page_owner[group_index, :, 0]
        pool_rows = jnp.arange(PAGES, dtype=jnp.int32) // PAGES_DEV * POOL_DEV + page_slot[group_index]
        paged_token_rows = cache_pool[owner_ids, pool_rows].reshape(PREFIX_SLOTS, KEYVALUE_WIDTH)
        every_key_row = jnp.concatenate([paged_token_rows[:, :key_value_split].reshape(PREFIX_SLOTS, KEYVALUE_HEADS, HEAD_SIZE), key_rotated], axis=0)
        every_value_row = jnp.concatenate([paged_token_rows[:, key_value_split:].reshape(PREFIX_SLOTS, KEYVALUE_HEADS, HEAD_SIZE), suffix_value], axis=0)
        prefix_seen = jnp.arange(PREFIX_SLOTS, dtype=jnp.int32) < prefix_length[group_index]
        causal = jnp.arange(SUFFIX_TOKENS)[None, :] <= jnp.arange(SUFFIX_TOKENS)[:, None]
        seen_mask = jnp.concatenate([jnp.broadcast_to(prefix_seen[None, :], (SUFFIX_TOKENS, PREFIX_SLOTS)), causal], axis=1)
        grouped_queries = query_rows.reshape(SUFFIX_TOKENS, KEYVALUE_HEADS, query_group_ratio, HEAD_SIZE)

        def head_portion(head_index):
            head_query = grouped_queries[:, head_index].reshape(SUFFIX_TOKENS * query_group_ratio, HEAD_SIZE)
            scores = jnp.dot(head_query, every_key_row[:, head_index].T, preferred_element_type=jnp.float32) * HEAD_SIZE ** (-0.5)
            scores = scores.reshape(SUFFIX_TOKENS, query_group_ratio, total_keys)
            scores = jnp.where(seen_mask[:, None, :], scores, floor_score)
            row_peak = lax.optimization_barrier(jnp.max(scores, axis=-1, keepdims=True))
            weights = jnp.where(seen_mask[:, None, :], jnp.exp(scores - row_peak), 0.0)
            totals = lax.optimization_barrier(jnp.sum(weights, axis=-1))
            numerator = jnp.dot(weights.astype(jnp.bfloat16).reshape(SUFFIX_TOKENS * query_group_ratio, total_keys), every_value_row[:, head_index], preferred_element_type=jnp.float32)
            return numerator.reshape(SUFFIX_TOKENS, query_group_ratio, HEAD_SIZE) / totals[..., None]
        split_per_head = lax.map(head_portion, jnp.arange(KEYVALUE_HEADS, dtype=jnp.int32))
        return split_per_head.transpose(1, 0, 2, 3).reshape(SUFFIX_TOKENS, QW).astype(jnp.bfloat16)
    return lax.map(one_group, jnp.arange(GROUPS, dtype=jnp.int32))
```

```python
import jax
import jax.numpy as jnp
from jax import lax
from jax.experimental import pallas as pl
from jax.experimental.pallas import tpu as pltpu
from jax.sharding import Mesh
from jax.sharding import PartitionSpec as P

MESH = pl.DeviceIdType.MESH
EPS = 1e-06
FLOOR = -1e30
GROUPS = 8
ROWS = 8
COLS = 4
CAP = 12
PAGES = 48
PAGE = 16
HEAD = 128
TOKENS = 16
RATIO = 8
KEYS = PAGES * PAGE
BLOCK = COLS * RATIO * TOKENS
HALF = BLOCK // 2
SUMROWS = 16
F32 = jnp.float32
BF16 = jnp.bfloat16


def rot(a, n):
    return lax.rem(a, jnp.int32(n))


def kernel(
    tab, cs, qraw, skv, qgain, kgain, plen, pool, out,
    send0, send1, send2, send3, recv0, recv1, recv2, recv3,
    kc, vc, vt, ks, vs, qsend, qbuf, oacc, mref, osend, stsend, orecv, strecv, fsend, frecv,
    reqv, reqs, idxv, idxs,
    psend, precv, lsem, rsend, rrecv, isend, irecv, ssem, xsend, xrecv,
    upsend, uprecv, dnsend, dnrecv, osem, orsem, tsem, trsem, fsem, frsem,
):
    g = lax.axis_index("group")
    z = lax.axis_index("ctx_0")
    x = lax.axis_index("ctx_1")
    sends = (send0, send1, send2, send3)
    recvs = (recv0, recv1, recv2, recv3)
    limit = plen[0]

    barrier = pltpu.get_barrier_semaphore()

    @pl.loop(1, GROUPS * COLS)
    def _(n):
        to = (rot(g + n // COLS, GROUPS), z, rot(x + rot(n, COLS), COLS))
        pl.semaphore_signal(barrier, inc=1, device_id=to, device_id_type=MESH)

    @pl.loop(1, ROWS)
    def _(n):
        pl.semaphore_signal(
            barrier, inc=1, device_id=(g, rot(z + n, ROWS), x), device_id_type=MESH
        )

    cosf = cs[0]
    sinf = cs[1]
    scale = HEAD ** (-0.5) * 1.4426950408889634

    def turned(raw, gain):
        raw = raw.astype(F32)
        mean = jnp.mean(raw * raw, axis=-1, keepdims=True)
        flat = raw * lax.rsqrt(mean + EPS) * gain
        return flat * cosf + pltpu.roll(flat, HEAD // 2, 1) * sinf

    for i in range(COLS * RATIO):
        part = turned(qraw[:, i * HEAD : (i + 1) * HEAD], qgain[...])
        qsend[i // RATIO, i % RATIO] = (part * scale).astype(BF16)
    for i in range(COLS):
        part = turned(skv[:, i * HEAD : (i + 1) * HEAD], kgain[...])
        qsend[i, RATIO] = part.astype(BF16)
        qsend[i, RATIO + 1] = skv[:, (COLS + i) * HEAD : (COLS + i + 1) * HEAD]

    pl.semaphore_wait(barrier, GROUPS * COLS - 1 + ROWS - 1)

    def req_copy(d):
        to = rot(g + d, GROUPS)
        return pltpu.make_async_remote_copy(
            src_ref=tab.at[to], dst_ref=reqv.at[g], send_sem=rsend.at[d], recv_sem=rrecv.at[d],
            device_id=(to, z, x), device_id_type=MESH,
        )

    def idx_copy(k):
        return pltpu.make_async_remote_copy(
            src_ref=tab.at[GROUPS], dst_ref=idxv.at[k], send_sem=isend.at[k], recv_sem=irecv.at[k],
            device_id=(g, z, rot(x + k, COLS)), device_id_type=MESH,
        )

    mine = z * COLS + x

    def q_copy(k):
        to = rot(x + k, COLS)
        return pltpu.make_async_remote_copy(
            src_ref=qsend.at[to], dst_ref=qbuf.at[mine], send_sem=xsend.at[k], recv_sem=xrecv.at[k],
            device_id=(g, z, to), device_id_type=MESH,
        )

    for d in range(1, GROUPS):
        req_copy(d).start()
    for k in range(1, COLS):
        idx_copy(k).start()
    for k in range(1, COLS):
        q_copy(k).start()

    def ring_copy(s, k, up):
        col = rot(x + COLS - k, COLS)
        away = rot(z + ROWS - s, ROWS) if up else rot(z + s, ROWS)
        place = away * COLS + col
        if s == 0 and k == 0:
            src = qsend.at[x, pl.ds(0, RATIO + 1)]
        else:
            src = qbuf.at[place, pl.ds(0, RATIO + 1)]
        to = rot(z + 1, ROWS) if up else rot(z + ROWS - 1, ROWS)
        return pltpu.make_async_remote_copy(
            src_ref=src, dst_ref=qbuf.at[place, pl.ds(0, RATIO + 1)],
            send_sem=(upsend if up else dnsend).at[s, k],
            recv_sem=(uprecv if up else dnrecv).at[s, k],
            device_id=(g, to, x), device_id_type=MESH,
        )

    ring_copy(0, 0, True).start()
    ring_copy(0, 0, False).start()
    qbuf[mine] = qsend[x]

    own_req = pltpu.make_async_copy(tab.at[g], reqs.at[g], ssem.at[0])
    own_idx = pltpu.make_async_copy(tab.at[GROUPS], idxs.at[0], ssem.at[GROUPS])
    own_req.start()
    own_idx.start()

    def req_local(d):
        frm = rot(g + GROUPS - d, GROUPS)
        return pltpu.make_async_copy(reqv.at[frm], reqs.at[frm], ssem.at[d])

    for d in range(1, GROUPS):
        req_copy(d).wait_recv()
        req_local(d).start()
    own_req.wait()
    for d in range(1, GROUPS):
        req_local(d).wait()

    def page_copy(k, d):
        to = rot(g + d, GROUPS)
        return pltpu.make_async_remote_copy(
            src_ref=sends[k].at[pl.ds(to * CAP, CAP)], dst_ref=recvs[k].at[pl.ds(g * CAP, CAP)],
            send_sem=psend.at[k, d], recv_sem=precv.at[k, d],
            device_id=(to, z, rot(x + k, COLS)), device_id_type=MESH,
        )

    own_pages = pltpu.make_async_copy(
        send0.at[pl.ds(g * CAP, CAP)], recv0.at[pl.ds(g * CAP, CAP)], lsem.at[0]
    )

    def gather(k):
        head = rot(x + k, COLS)
        key_at = pl.multiple_of(head * HEAD, HEAD)
        value_at = pl.multiple_of((COLS + head) * HEAD, HEAD)

        @pl.loop(0, GROUPS)
        def _(d):
            to = rot(g + d, GROUPS)
            for r in range(CAP):
                slot = reqs[to, 0, r]
                sends[k][to * CAP + r, :, 0:HEAD] = pool[slot, :, pl.ds(key_at, HEAD)]
                sends[k][to * CAP + r, :, HEAD : 2 * HEAD] = pool[slot, :, pl.ds(value_at, HEAD)]
            if k:
                page_copy(k, d).start()
            else:

                @pl.when(d > 0)
                def _():
                    page_copy(0, d).start()

    for k in range(COLS):
        gather(k)
    own_pages.start()

    for k in range(1, COLS):
        q_copy(k).wait_recv()
        ring_copy(0, k, True).start()
        ring_copy(0, k, False).start()
    for s in range(1, 5):
        for k in range(COLS):
            ring_copy(s - 1, k, True).wait_recv()
            if s < 4:
                ring_copy(s, k, True).start()
            if s < 4:
                ring_copy(s - 1, k, False).wait_recv()
            if s < 3:
                ring_copy(s, k, False).start()

    for k in range(1, COLS):
        idx_copy(k).wait_recv()
        pltpu.make_async_copy(idxv.at[k], idxs.at[k], ssem.at[GROUPS + k]).start()
    own_idx.wait()
    for k in range(1, COLS):
        pltpu.make_async_copy(idxv.at[k], idxs.at[k], ssem.at[GROUPS + k]).wait()

    def queries(zb, c):
        part = qbuf[pl.ds(zb * COLS + 2 * c, 2), 0:RATIO]
        return part.reshape(HALF, HEAD)

    def logits(keys, zb, c):
        return lax.dot_general(
            keys, queries(zb, c), (((1,), (1,)), ((), ())), preferred_element_type=F32
        )

    for b in range(COLS):
        ks[b * TOKENS : (b + 1) * TOKENS] = qbuf[z * COLS + b, RATIO]
        vs[b * TOKENS : (b + 1) * TOKENS] = qbuf[z * COLS + b, RATIO + 1].astype(F32)
    ks[COLS * TOKENS :] = jnp.zeros((HEAD - COLS * TOKENS, HEAD), BF16)
    vs[COLS * TOKENS :] = jnp.zeros((HEAD - COLS * TOKENS, HEAD), F32)
    suffix_t = jnp.concatenate(
        [vs[...].T.astype(BF16), jnp.ones((SUMROWS, HEAD), BF16)], axis=0
    )
    suffix_k = ks[...]

    @pl.loop(0, ROWS)
    def _(zb):
        for c in range(2):
            key_row = lax.broadcasted_iota(jnp.int32, (HEAD, HALF), 0)
            column = lax.broadcasted_iota(jnp.int32, (HEAD, HALF), 1)
            asker = zb * (COLS * TOKENS) + (column // HEAD + 2 * c) * TOKENS + (column & (TOKENS - 1))
            seen = (key_row < COLS * TOKENS) & (z * (COLS * TOKENS) + key_row <= asker)
            s = jnp.where(seen, logits(suffix_k, zb, c), FLOOR)
            peak = jnp.max(s, axis=0, keepdims=True)
            p = jnp.exp2(s - peak).astype(BF16)
            at = slice(c * HALF, (c + 1) * HALF)
            mref[zb, 0:1, at] = peak
            oacc[zb, :, at] = jnp.dot(suffix_t, p, preferred_element_type=F32)

    shared_key = qbuf[0, RATIO][0:1, :].astype(F32)

    def compact(k):
        col = rot(x + COLS - k, COLS)
        base = (z * COLS + col) * KEYS

        @pl.loop(0, PAGES)
        def _(j):
            page = recvs[k][idxs[k, 0, j]].astype(F32)
            token = base + j * PAGE + lax.broadcasted_iota(jnp.int32, (PAGE, HEAD), 0)
            seen = token < limit
            rows = pl.ds(pl.multiple_of(j * PAGE, PAGE), PAGE)
            kc[rows, :] = jnp.where(seen, page[:, 0:HEAD], shared_key).astype(BF16)
            vc[rows, :] = jnp.where(seen, page[:, HEAD:], 0.0)

        lane = base + lax.broadcasted_iota(jnp.int32, (SUMROWS, KEYS), 1)
        for b in range(KEYS // HEAD):
            vt[0:HEAD, b * HEAD : (b + 1) * HEAD] = vc[b * HEAD : (b + 1) * HEAD, :].T.astype(BF16)
        vt[HEAD:, :] = jnp.where(lane < limit, 1.0, 0.0).astype(BF16)

    def attend(zb):
        for c in range(2):
            at = slice(c * HALF, (c + 1) * HALF)
            s = logits(kc[...], zb, c)
            before = mref[zb, 0:1, at]
            peak = jnp.maximum(before, jnp.max(s, axis=0, keepdims=True))
            p = jnp.exp2(s - peak).astype(BF16)
            fresh = jnp.dot(vt[...], p, preferred_element_type=F32)
            oacc[zb, :, at] = oacc[zb, :, at] * jnp.exp2(before - peak) + fresh
            mref[zb, 0:1, at] = peak

    def o_copy(off):
        to = rot(z + off, ROWS)
        return pltpu.make_async_remote_copy(
            src_ref=osend.at[to], dst_ref=orecv.at[off], send_sem=osem.at[off], recv_sem=orsem.at[off],
            device_id=(g, to, x), device_id_type=MESH,
        )

    def t_copy(off):
        to = rot(z + off, ROWS)
        return pltpu.make_async_remote_copy(
            src_ref=stsend.at[to], dst_ref=strecv.at[off], send_sem=tsem.at[off], recv_sem=trsem.at[off],
            device_id=(g, to, x), device_id_type=MESH,
        )

    for k in range(COLS):
        if k == 0:
            own_pages.wait()
        for d in range(0 if k else 1, GROUPS):
            page_copy(k, d).wait_recv()
        compact(k)
        if k < COLS - 1:

            @pl.loop(0, ROWS)
            def _(zb):
                attend(zb)

        else:

            @pl.loop(0, ROWS)
            def _(n):
                off = 4 + (1 - 2 * rot(n, 2)) * ((n + 1) // 2)
                zb = rot(z + off, ROWS)
                attend(zb)
                osend[zb] = oacc[zb, 0:HEAD, :].astype(BF16)
                stsend[zb, 0:1, :] = mref[zb, 0:1, :]
                stsend[zb, 1:2, :] = oacc[zb, HEAD : HEAD + 1, :]

                @pl.when(n < ROWS - 1)
                def _():
                    t_copy(off).start()
                    o_copy(off).start()

    for off in range(1, ROWS):
        t_copy(off).wait_recv()
    peaks = [stsend[z, 0:1, :]] + [strecv[off, 0:1, :] for off in range(1, ROWS)]
    sums = [stsend[z, 1:2, :]] + [strecv[off, 1:2, :] for off in range(1, ROWS)]
    top = peaks[0]
    for off in range(1, ROWS):
        top = jnp.maximum(top, peaks[off])
    parts = [jnp.exp2(peak - top) for peak in peaks]
    total = parts[0] * sums[0]
    for off in range(1, ROWS):
        total = total + parts[off] * sums[off]
    joined = osend[z].astype(F32) * parts[0]
    for off in (1, 7, 2, 6, 3, 5, 4):
        o_copy(off).wait_recv()
        joined = joined + orecv[off].astype(F32) * parts[off]
    joined = joined / total
    for b in range(COLS):
        block = joined[:, b * HEAD : (b + 1) * HEAD].T.astype(BF16)
        fsend[b] = block.reshape(RATIO, TOKENS, HEAD)

    def f_copy(k):
        to = rot(x + k, COLS)
        return pltpu.make_async_remote_copy(
            src_ref=fsend.at[to], dst_ref=frecv.at[x], send_sem=fsem.at[k], recv_sem=frsem.at[k],
            device_id=(g, z, to), device_id_type=MESH,
        )

    for k in range(1, COLS):
        f_copy(k).start()
    frecv[x] = fsend[x]
    for k in range(1, COLS):
        f_copy(k).wait_recv()
    for h in range(COLS):
        for i in range(RATIO):
            at = (h * RATIO + i) * HEAD
            out[:, at : at + HEAD] = frecv[h, i]

    for d in range(1, GROUPS):
        req_copy(d).wait_send()
    for k in range(1, COLS):
        idx_copy(k).wait_send()
        q_copy(k).wait_send()
        f_copy(k).wait_send()
    for s in range(4):
        for k in range(COLS):
            ring_copy(s, k, True).wait_send()
            if s < 3:
                ring_copy(s, k, False).wait_send()
    for k in range(COLS):
        for d in range(0 if k else 1, GROUPS):
            page_copy(k, d).wait_send()
    for off in range(1, ROWS):
        t_copy(off).wait_send()
        o_copy(off).wait_send()


def shards(
    query_raw, suffix_keyval, query_gain, key_norm_gain, positions, prefix_length,
    page_owner, page_slot, cache_pool,
):
    half = HEAD // 2
    frequency = 1000000.0 ** (-(2.0 / HEAD) * jnp.arange(half, dtype=F32))
    angles = positions[0].astype(F32)[:, None] * frequency[None, :]
    cosine, sine = jnp.cos(angles), jnp.sin(angles)
    cs = jnp.stack(
        [jnp.concatenate([cosine, cosine], axis=1), jnp.concatenate([-sine, sine], axis=1)]
    )
    owner = page_owner[0, :, 0]
    slot = page_slot[0]
    order = jnp.arange(PAGES, dtype=jnp.int32)
    same = (owner[:, None] == owner[None, :]) & (order[None, :] < order[:, None])
    place = owner * CAP + jnp.sum(same.astype(jnp.int32), axis=1)
    lanes = jnp.arange(HEAD, dtype=jnp.int32)
    wanted = jnp.where(
        lanes < CAP, jnp.arange(GROUPS, dtype=jnp.int32)[:, None] * CAP + lanes[None, :], -1
    )
    hit = wanted[:, :, None] == place[None, None, :]
    requests = jnp.sum(jnp.where(hit, slot[None, None, :], 0), axis=2)
    places = jnp.pad(place, (0, HEAD - PAGES))[None]
    tab = jnp.concatenate([requests, places], axis=0)
    tab = jnp.broadcast_to(tab[:, None, :], (GROUPS + 1, 8, HEAD))
    vmem = pl.BlockSpec(memory_space=pltpu.VMEM)
    page_half = (GROUPS * CAP, PAGE, 2 * HEAD)
    dma = pltpu.SemaphoreType.DMA
    result = pl.pallas_call(
        kernel,
        out_shape=jax.ShapeDtypeStruct((TOKENS, COLS * RATIO * HEAD), BF16),
        in_specs=[vmem] * 6 + [pl.BlockSpec(memory_space=pltpu.SMEM), vmem],
        out_specs=vmem,
        scratch_shapes=[pltpu.VMEM(page_half, BF16)] * 8
        + [
            pltpu.VMEM((KEYS, HEAD), BF16),
            pltpu.VMEM((KEYS, HEAD), F32),
            pltpu.VMEM((HEAD + SUMROWS, KEYS), BF16),
            pltpu.VMEM((HEAD, HEAD), BF16),
            pltpu.VMEM((HEAD, HEAD), F32),
            pltpu.VMEM((COLS, RATIO + 2, TOKENS, HEAD), BF16),
            pltpu.VMEM((ROWS * COLS, RATIO + 2, TOKENS, HEAD), BF16),
            pltpu.VMEM((ROWS, HEAD + SUMROWS, BLOCK), F32),
            pltpu.VMEM((ROWS, 8, BLOCK), F32),
            pltpu.VMEM((ROWS, HEAD, BLOCK), BF16),
            pltpu.VMEM((ROWS, 8, BLOCK), F32),
            pltpu.VMEM((ROWS, HEAD, BLOCK), BF16),
            pltpu.VMEM((ROWS, 8, BLOCK), F32),
            pltpu.VMEM((COLS, RATIO, TOKENS, HEAD), BF16),
            pltpu.VMEM((COLS, RATIO, TOKENS, HEAD), BF16),
            pltpu.VMEM((GROUPS, 8, HEAD), jnp.int32),
            pltpu.SMEM((GROUPS, 8, HEAD), jnp.int32),
            pltpu.VMEM((COLS, 8, HEAD), jnp.int32),
            pltpu.SMEM((COLS, 8, HEAD), jnp.int32),
            dma((COLS, GROUPS)), dma((COLS, GROUPS)), dma((1,)),
            dma((GROUPS,)), dma((GROUPS,)), dma((COLS,)), dma((COLS,)), dma((GROUPS + COLS,)),
            dma((COLS,)), dma((COLS,)),
            dma((4, COLS)), dma((4, COLS)), dma((3, COLS)), dma((3, COLS)),
            dma((ROWS,)), dma((ROWS,)), dma((ROWS,)), dma((ROWS,)),
            dma((COLS,)), dma((COLS,)),
        ],
        compiler_params=pltpu.CompilerParams(
            collective_id=0, has_side_effects=True, vmem_limit_bytes=60 * 1024 * 1024
        ),
        name="spanned",
    )(
        tab, cs, query_raw[0], suffix_keyval[0], query_gain[None], key_norm_gain[None],
        prefix_length, cache_pool[0],
    )
    return result[None]


def solution(mesh):
    finer = Mesh(mesh.devices.reshape(GROUPS, ROWS, COLS), ("group", "ctx_0", "ctx_1"))
    ctx = ("ctx_0", "ctx_1")
    in_specs = (
        P("group", ctx, None),
        P("group", ctx, None),
        P(),
        P(),
        P("group", ctx),
        P("group"),
        P("group", ctx, None),
        P("group", ctx),
        P("group", ctx, None, None),
    )
    return jax.shard_map(
        shards, mesh=finer, in_specs=in_specs, out_specs=P("group", ctx, None), check_vma=False
    )
```

```python
import jax
import jax.numpy as jnp
from jax import lax
from jax.experimental import pallas as pl
from jax.experimental.pallas import tpu as pltpu
from jax.sharding import Mesh
from jax.sharding import PartitionSpec as P

MESH = pl.DeviceIdType.MESH
EPS = 1e-06
FLOOR = -65536.0
GROUPS = 8
ROWS = 8
COLS = 4
CAP = 12
PAGES = 48
POOL = 96
PAGE = 16
HEAD = 128
TOKENS = 16
RATIO = 8
KEYS = PAGES * PAGE
BLOCK = COLS * RATIO * TOKENS
HALF = BLOCK // 2
SUMROWS = 16
WIDE = KEYS + HEAD
LAST = (4, 5, 3, 6, 2, 7, 1, 0)
F32 = jnp.float32
BF16 = jnp.bfloat16


def rot(a, n):
    return lax.rem(a, jnp.int32(n))


def kernel(
    tab, cs, qraw, skv, qgain, kgain, plen, pool_any, out,
    pool, send0, send1, send2, send3, recv0, recv1, recv2, recv3,
    near0, near1, near2, near3, cut1, cut2, cut3,
    kc, vt, sa, sb, pa, pb, qsend, qbuf, oacc, mref, osend, upin, dnin, fsend, frecv,
    reqv, reqs, idxs,
    psend, precv, lsem, rsend, rrecv, ssem, xsend, xrecv,
    upsend, uprecv, dnsend, dnrecv, nsend, nrecv, uosend, uorecv, dosend, dorecv, fsem, frsem,
):
    g = lax.axis_index("group")
    z = lax.axis_index("ctx_0")
    x = lax.axis_index("ctx_1")
    sends = (send0, send1, send2, send3)
    recvs = (recv0, recv1, recv2, recv3)
    nears = (near0, near1, near2, near3)
    cuts = (near0, cut1, cut2, cut3)
    limit = plen[0]
    up_z, down_z = rot(z + 1, ROWS), rot(z + ROWS - 1, ROWS)

    load_pool = pltpu.make_async_copy(pool_any, pool, lsem.at[COLS])
    load_pool.start()
    barrier = pltpu.get_barrier_semaphore()
    partners = [(rot(g + n, GROUPS), z, x) for n in range(1, GROUPS)]
    partners += [(g, z, rot(x + n, COLS)) for n in range(1, COLS)]
    partners += [(g, up_z, x), (g, down_z, x)]
    for to in partners:
        pl.semaphore_signal(barrier, inc=1, device_id=to, device_id_type=MESH)

    cosf = cs[0]
    sinf = cs[1]
    scale = HEAD ** (-0.5) * 1.4426950408889634

    def turned(raw, gain):
        raw = raw.astype(F32)
        mean = jnp.mean(raw * raw, axis=-1, keepdims=True)
        flat = raw * lax.rsqrt(mean + EPS) * gain
        return flat * cosf + pltpu.roll(flat, HEAD // 2, 1) * sinf

    for i in range(COLS * RATIO):
        part = turned(qraw[:, i * HEAD : (i + 1) * HEAD], qgain[...])
        qsend[i // RATIO, i % RATIO] = (part * scale).astype(BF16)
    for i in range(COLS):
        part = turned(skv[:, i * HEAD : (i + 1) * HEAD], kgain[...])
        qsend[i, RATIO] = part.astype(BF16)
        qsend[i, RATIO + 1] = skv[:, (COLS + i) * HEAD : (COLS + i + 1) * HEAD]

    pl.semaphore_wait(barrier, len(partners))

    def req_copy(d):
        to = rot(g + d, GROUPS)
        return pltpu.make_async_remote_copy(
            src_ref=tab.at[to], dst_ref=reqv.at[g], send_sem=rsend.at[d], recv_sem=rrecv.at[d],
            device_id=(to, z, x), device_id_type=MESH,
        )

    mine = z * COLS + x

    def q_copy(k):
        to = rot(x + k, COLS)
        return pltpu.make_async_remote_copy(
            src_ref=qsend.at[to], dst_ref=qbuf.at[mine], send_sem=xsend.at[k], recv_sem=xrecv.at[k],
            device_id=(g, z, to), device_id_type=MESH,
        )

    for d in range(1, GROUPS):
        req_copy(d).start()
    for k in range(1, COLS):
        q_copy(k).start()

    def ring_copy(s, k, up):
        col = rot(x + COLS - k, COLS)
        away = rot(z + ROWS - s, ROWS) if up else rot(z + s, ROWS)
        place = away * COLS + col
        if s == 0 and k == 0:
            src = qsend.at[x, pl.ds(0, RATIO + 1)]
        else:
            src = qbuf.at[place, pl.ds(0, RATIO + 1)]
        return pltpu.make_async_remote_copy(
            src_ref=src, dst_ref=qbuf.at[place, pl.ds(0, RATIO + 1)],
            send_sem=(upsend if up else dnsend).at[s, k],
            recv_sem=(uprecv if up else dnrecv).at[s, k],
            device_id=(g, up_z if up else down_z, x), device_id_type=MESH,
        )

    ring_copy(0, 0, True).start()
    ring_copy(0, 0, False).start()
    qbuf[mine] = qsend[x]

    own_req = pltpu.make_async_copy(tab.at[g], reqs.at[g], ssem.at[0])
    own_idx = pltpu.make_async_copy(tab.at[GROUPS], idxs, ssem.at[GROUPS])
    own_req.start()
    own_idx.start()

    def req_local(d):
        frm = rot(g + GROUPS - d, GROUPS)
        return pltpu.make_async_copy(reqv.at[frm], reqs.at[frm], ssem.at[d])

    for d in range(1, GROUPS):
        req_copy(d).wait_recv()
        req_local(d).start()
    own_req.wait()
    own_idx.wait()
    for d in range(1, GROUPS):
        req_local(d).wait()
    load_pool.wait()

    def page_copy(k, d):
        to = rot(g + d, GROUPS)
        return pltpu.make_async_remote_copy(
            src_ref=sends[k].at[pl.ds(to * CAP, CAP)], dst_ref=recvs[k].at[pl.ds(g * CAP, CAP)],
            send_sem=psend.at[k, d], recv_sem=precv.at[k, d],
            device_id=(to, z, x), device_id_type=MESH,
        )

    def own_pages(k):
        own = pl.ds(g * CAP, CAP)
        return pltpu.make_async_copy(sends[k].at[own], recvs[k].at[own], lsem.at[k])

    def gather(k):
        head = rot(x + k, COLS)
        key_at = pl.multiple_of(head * HEAD, HEAD)
        value_at = pl.multiple_of((COLS + head) * HEAD, HEAD)

        @pl.loop(0, GROUPS)
        def _(d):
            to = rot(g + d, GROUPS)
            for r in range(CAP):
                slot = reqs[to, 0, r]
                sends[k][to * CAP + r, :, 0:HEAD] = pool[slot, :, pl.ds(key_at, HEAD)]
                sends[k][to * CAP + r, :, HEAD : 2 * HEAD] = pool[slot, :, pl.ds(value_at, HEAD)]

            @pl.when(d > 0)
            def _():
                page_copy(k, d).start()

        own_pages(k).start()

    for k in (1, 2, 3, 0):
        gather(k)

    def near_copy(k):
        return pltpu.make_async_remote_copy(
            src_ref=cuts[k], dst_ref=nears[k], send_sem=nsend.at[k], recv_sem=nrecv.at[k],
            device_id=(g, z, rot(x + k, COLS)), device_id_type=MESH,
        )

    def compact(k):
        for d in range(1, GROUPS):
            page_copy(k, d).wait_recv()
        own_pages(k).wait()

        @pl.loop(0, PAGES // 4)
        def _(j):
            for i in range(4):
                rows = pl.ds(pl.multiple_of((j * 4 + i) * PAGE, PAGE), PAGE)
                cuts[k][rows, :] = recvs[k][idxs[0, j * 4 + i]]

        if k:
            near_copy(k).start()

    for k in range(1, COLS):
        q_copy(k).wait_recv()
        ring_copy(0, k, True).start()
        ring_copy(0, k, False).start()
    for s in range(1, 5):
        for k in range(COLS):
            ring_copy(s - 1, k, True).wait_recv()
            if s < 4:
                ring_copy(s, k, True).start()
            if s < 4:
                ring_copy(s - 1, k, False).wait_recv()
            if s < 3:
                ring_copy(s, k, False).start()
        if s == 2:
            compact(1)

    def queries(zb, c):
        part = qbuf[pl.ds(zb * COLS + 2 * c, 2), 0:RATIO]
        return part.reshape(HALF, HEAD)

    for b in range(COLS):
        rows = slice(KEYS + b * TOKENS, KEYS + (b + 1) * TOKENS)
        kc[rows, :] = qbuf[z * COLS + b, RATIO]
    kc[KEYS + COLS * TOKENS :, :] = jnp.zeros((HEAD - COLS * TOKENS, HEAD), BF16)
    suffix_v = [qbuf[z * COLS + b, RATIO + 1].astype(F32) for b in range(COLS)]
    suffix_v = jnp.concatenate(suffix_v + [jnp.zeros((HEAD - COLS * TOKENS, HEAD), F32)], axis=0)
    vt[0:HEAD, KEYS:] = suffix_v.T.astype(BF16)
    vt[HEAD:, KEYS:] = jnp.ones((SUMROWS, HEAD), BF16)

    shared_key = qbuf[0, RATIO][0:1, :].astype(F32)

    def prepare(k):
        base = (z * COLS + rot(x + COLS - k, COLS)) * KEYS
        for b in range(KEYS // HEAD):
            rows = slice(b * HEAD, (b + 1) * HEAD)
            token = base + b * HEAD + lax.broadcasted_iota(jnp.int32, (HEAD, HEAD), 0)
            seen = token < limit
            keys = nears[k][rows, 0:HEAD].astype(F32)
            values = nears[k][rows, HEAD:].astype(F32)
            kc[rows, :] = jnp.where(seen, keys, shared_key).astype(BF16)
            vt[0:HEAD, rows] = jnp.where(seen, values, 0.0).T.astype(BF16)
        lane = base + lax.broadcasted_iota(jnp.int32, (SUMROWS, KEYS), 1)
        vt[HEAD:, 0:KEYS] = jnp.where(lane < limit, 1.0, 0.0).astype(BF16)

    def scores(dst, peak, zb, c, first):
        size = WIDE if first else KEYS
        s = lax.dot_general(
            kc[0:size, :], queries(zb, c), (((1,), (1,)), ((), ())), preferred_element_type=F32
        )
        if first:
            key_row = lax.broadcasted_iota(jnp.int32, (HEAD, HALF), 0)
            column = lax.broadcasted_iota(jnp.int32, (HEAD, HALF), 1)
            asker = zb * (COLS * TOKENS) + (column // HEAD + 2 * c) * TOKENS + (column & (TOKENS - 1))
            seen = (key_row < COLS * TOKENS) & (z * (COLS * TOKENS) + key_row <= asker)
            own = jnp.where(seen, s[KEYS:], FLOOR)
            dst[KEYS:, :] = own
            s = s[0:KEYS]
        dst[0:KEYS, :] = s
        top = jnp.max(s, axis=0, keepdims=True)
        if first:
            top = jnp.maximum(top, jnp.max(own, axis=0, keepdims=True))
        peak[0:1, :] = jnp.ceil(top * 0.25) * 4.0

    def finish(src, peak, zb, c, first):
        size = WIDE if first else KEYS
        at = slice(c * HALF, (c + 1) * HALF)
        top = peak[0:1, :]
        if not first:
            before = mref[zb, 0:1, at]
            top = jnp.maximum(before, top)
        p = jnp.exp2(src[0:size, :] - top).astype(BF16)
        fresh = jnp.dot(vt[:, 0:size], p, preferred_element_type=F32)
        if not first:
            fresh = oacc[zb, :, at] * jnp.exp2(before - top) + fresh
        oacc[zb, :, at] = fresh
        mref[zb, 0:1, at] = top

    def attend(k, first):
        if k:
            near_copy(k).wait_recv()
        prepare(k)
        scores(sa, pa, 0, 0, first)

        @pl.loop(0, ROWS)
        def _(zb):
            scores(sb, pb, zb, 1, first)
            finish(sa, pa, zb, 0, first)
            scores(sa, pa, jnp.minimum(zb + 1, ROWS - 1), 0, first)
            finish(sb, pb, zb, 1, first)

    def sum_copy(s, q, up):
        block = rot(z + 4 - s, ROWS) if up else rot(z + 5 + s, ROWS)
        return pltpu.make_async_remote_copy(
            src_ref=osend.at[block, q], dst_ref=(upin if up else dnin).at[s, q],
            send_sem=(uosend if up else dosend).at[s, q],
            recv_sem=(uorecv if up else dorecv).at[s, q],
            device_id=(g, up_z if up else down_z, x), device_id_type=MESH,
        )

    def own_part(zb, q):
        at = slice(q * HEAD, (q + 1) * HEAD)
        return oacc[zb, 0:HEAD, at], mref[zb, 0:1, at], oacc[zb, HEAD : HEAD + 1, at]

    def join(part, arrived):
        o, m, l = part
        tile = arrived[HEAD:, :].astype(F32)
        m_in = tile[0:1]
        l_in = tile[1:2] + tile[2:3]
        top = jnp.maximum(m, m_in)
        mul, mul_in = jnp.exp2(m - top), jnp.exp2(m_in - top)
        return o * mul + arrived[0:HEAD, :].astype(F32) * mul_in, top, l * mul + l_in * mul_in

    def pack(zb, q, part):
        o, m, l = part
        l_high = l.astype(BF16).astype(F32)
        row = lax.broadcasted_iota(jnp.int32, (SUMROWS, HEAD), 0)
        tile = jnp.where(row == 0, m, jnp.where(row == 1, l_high, jnp.where(row == 2, l - l_high, 0.0)))
        osend[zb, q, 0:HEAD, :] = o.astype(BF16)
        osend[zb, q, HEAD:, :] = tile.astype(BF16)

    def relay(s, up):
        block = rot(z + 4 - s, ROWS) if up else rot(z + 5 + s, ROWS)
        for q in range(COLS):
            part = own_part(block, q)
            if s:
                sum_copy(s - 1, q, up).wait_recv()
                part = join(part, (upin if up else dnin).at[s - 1, q])
            pack(block, q, part)
            sum_copy(s, q, up).start()

    def f_copy(q, k):
        return pltpu.make_async_remote_copy(
            src_ref=fsend.at[q], dst_ref=frecv.at[x], send_sem=fsem.at[k], recv_sem=frsem.at[k],
            device_id=(g, z, q), device_id_type=MESH,
        )

    compact(2)
    attend(1, True)
    compact(3)
    attend(2, False)
    attend(3, False)
    compact(0)
    prepare(0)

    def block_at(n):
        return rot(z + LAST[n], ROWS)

    scores(sa, pa, block_at(0), 0, False)
    for n in range(ROWS):
        scores(sb, pb, block_at(n), 1, False)
        finish(sa, pa, block_at(n), 0, False)
        if n < ROWS - 1:
            scores(sa, pa, block_at(n + 1), 0, False)
        finish(sb, pb, block_at(n), 1, False)
        if n == 0:
            relay(0, True)
        if n == 1:
            relay(0, False)
        if n in (3, 5):
            relay(n // 2, True)
            relay(n // 2, False)
    relay(3, True)

    for q in range(COLS):
        part = own_part(z, q)
        sum_copy(2, q, False).wait_recv()
        part = join(part, dnin.at[2, q])
        sum_copy(3, q, True).wait_recv()
        o, m, l = join(part, upin.at[3, q])
        fsend[q] = (o / l).T.astype(BF16).reshape(RATIO, TOKENS, HEAD)
        k = rot(q + COLS - x, COLS)

        @pl.when(k > 0)
        def _():
            f_copy(q, k).start()

    frecv[x] = fsend[x]
    for k in range(1, COLS):
        f_copy(rot(x + k, COLS), k).wait_recv()
    for h in range(COLS):
        for i in range(RATIO):
            at = (h * RATIO + i) * HEAD
            out[:, at : at + HEAD] = frecv[h, i]

    for d in range(1, GROUPS):
        req_copy(d).wait_send()
    for k in range(1, COLS):
        q_copy(k).wait_send()
        near_copy(k).wait_send()
        f_copy(rot(x + k, COLS), k).wait_send()
    for s in range(4):
        for k in range(COLS):
            ring_copy(s, k, True).wait_send()
            sum_copy(s, k, True).wait_send()
            if s < 3:
                ring_copy(s, k, False).wait_send()
                sum_copy(s, k, False).wait_send()
    for k in range(COLS):
        for d in range(1, GROUPS):
            page_copy(k, d).wait_send()


def shards(
    query_raw, suffix_keyval, query_gain, key_norm_gain, positions, prefix_length,
    page_owner, page_slot, cache_pool,
):
    half = HEAD // 2
    frequency = 1000000.0 ** (-(2.0 / HEAD) * jnp.arange(half, dtype=F32))
    angles = positions[0].astype(F32)[:, None] * frequency[None, :]
    cosine, sine = jnp.cos(angles), jnp.sin(angles)
    cs = jnp.stack(
        [jnp.concatenate([cosine, cosine], axis=1), jnp.concatenate([-sine, sine], axis=1)]
    )
    owner = page_owner[0, :, 0]
    slot = page_slot[0]
    order = jnp.arange(PAGES, dtype=jnp.int32)
    same = (owner[:, None] == owner[None, :]) & (order[None, :] < order[:, None])
    place = owner * CAP + jnp.sum(same.astype(jnp.int32), axis=1)
    lanes = jnp.arange(HEAD, dtype=jnp.int32)
    wanted = jnp.where(
        lanes < CAP, jnp.arange(GROUPS, dtype=jnp.int32)[:, None] * CAP + lanes[None, :], -1
    )
    hit = wanted[:, :, None] == place[None, None, :]
    requests = jnp.sum(jnp.where(hit, slot[None, None, :], 0), axis=2)
    places = jnp.pad(place, (0, HEAD - PAGES))[None]
    tab = jnp.concatenate([requests, places], axis=0)
    tab = jnp.broadcast_to(tab[:, None, :], (GROUPS + 1, 8, HEAD))
    vmem = pl.BlockSpec(memory_space=pltpu.VMEM)
    page_half = (GROUPS * CAP, PAGE, 2 * HEAD)
    dma = pltpu.SemaphoreType.DMA
    result = pl.pallas_call(
        kernel,
        out_shape=jax.ShapeDtypeStruct((TOKENS, COLS * RATIO * HEAD), BF16),
        in_specs=[vmem] * 6
        + [pl.BlockSpec(memory_space=pltpu.SMEM), pl.BlockSpec(memory_space=pl.ANY)],
        out_specs=vmem,
        scratch_shapes=[pltpu.VMEM((POOL, PAGE, 2 * COLS * HEAD), BF16)]
        + [pltpu.VMEM(page_half, BF16)] * 8
        + [pltpu.VMEM((KEYS, 2 * HEAD), BF16)] * 7
        + [
            pltpu.VMEM((WIDE, HEAD), BF16),
            pltpu.VMEM((HEAD + SUMROWS, WIDE), BF16),
            pltpu.VMEM((WIDE, HALF), F32),
            pltpu.VMEM((WIDE, HALF), F32),
            pltpu.VMEM((8, HALF), F32),
            pltpu.VMEM((8, HALF), F32),
            pltpu.VMEM((COLS, RATIO + 2, TOKENS, HEAD), BF16),
            pltpu.VMEM((ROWS * COLS, RATIO + 2, TOKENS, HEAD), BF16),
            pltpu.VMEM((ROWS, HEAD + SUMROWS, BLOCK), F32),
            pltpu.VMEM((ROWS, 8, BLOCK), F32),
            pltpu.VMEM((ROWS, COLS, HEAD + SUMROWS, HEAD), BF16),
            pltpu.VMEM((4, COLS, HEAD + SUMROWS, HEAD), BF16),
            pltpu.VMEM((3, COLS, HEAD + SUMROWS, HEAD), BF16),
            pltpu.VMEM((COLS, RATIO, TOKENS, HEAD), BF16),
            pltpu.VMEM((COLS, RATIO, TOKENS, HEAD), BF16),
            pltpu.VMEM((GROUPS, 8, HEAD), jnp.int32),
            pltpu.SMEM((GROUPS, 8, HEAD), jnp.int32),
            pltpu.SMEM((8, HEAD), jnp.int32),
            dma((COLS, GROUPS)), dma((COLS, GROUPS)), dma((COLS + 1,)),
            dma((GROUPS,)), dma((GROUPS,)), dma((GROUPS + 1,)),
            dma((COLS,)), dma((COLS,)),
            dma((4, COLS)), dma((4, COLS)), dma((3, COLS)), dma((3, COLS)),
            dma((COLS,)), dma((COLS,)),
            dma((4, COLS)), dma((4, COLS)), dma((3, COLS)), dma((3, COLS)),
            dma((COLS,)), dma((COLS,)),
        ],
        compiler_params=pltpu.CompilerParams(
            collective_id=0, has_side_effects=True, vmem_limit_bytes=60 * 1024 * 1024
        ),
        name="spanned",
    )(
        tab, cs, query_raw[0], suffix_keyval[0], query_gain[None], key_norm_gain[None],
        prefix_length, cache_pool[0],
    )
    return result[None]


def solution(mesh):
    finer = Mesh(mesh.devices.reshape(GROUPS, ROWS, COLS), ("group", "ctx_0", "ctx_1"))
    ctx = ("ctx_0", "ctx_1")
    in_specs = (
        P("group", ctx, None),
        P("group", ctx, None),
        P(),
        P(),
        P("group", ctx),
        P("group"),
        P("group", ctx, None),
        P("group", ctx),
        P("group", ctx, None, None),
    )
    return jax.shard_map(
        shards, mesh=finer, in_specs=in_specs, out_specs=P("group", ctx, None), check_vma=False
    )
```

```python
import jax
import jax.numpy as jnp
import numpy as np
from jax import lax
from jax.experimental import pallas as pl
from jax.experimental.pallas import tpu as pltpu
from jax.sharding import Mesh
from jax.sharding import PartitionSpec as P

MESH = pl.DeviceIdType.MESH
EPS = 1e-06
FLOOR = -65536.0
GROUPS = 8
ROWS = 8
COLS = 4
CAP = 12
PAGES = 48
POOL = 96
PAGE = 16
HEAD = 128
TOKENS = 16
RATIO = 8
KEYS = PAGES * PAGE
BLOCK = COLS * RATIO * TOKENS
HALF = BLOCK // 2
SUMROWS = 16
WIDE = KEYS + HEAD
CUT = 384
LAST = (4, 3, 5, 2, 6, 1, 7, 0)
QUARTERS = (2, 1, 3, 0)
FIRST_UP = (0, 1)
FIRST_DOWN = (2, 3)
F32 = jnp.float32
BF16 = jnp.bfloat16


def rot(a, n):
    return lax.rem(a, jnp.int32(n))


def kernel(
    owner, slots, freq, qraw_any, skv_any, qgain, kgain, plen, pool_any, out,
    qraw, skv, mix, tab, pool, send0, send1, send2, send3, recv0, recv1, recv2, recv3,
    near0, near1, near2, near3, cut1, cut2, cut3,
    kc, vt, sa, sb, pa, pb, qsend, qbuf, oacc, mref, osend, upin, dnin, fsend, frecv,
    reqv, reqs,
    psend, precv, lsem, rsend, rrecv, ssem, xsend, xrecv,
    upsend, uprecv, dnsend, dnrecv, nsend, nrecv, uosend, uorecv, dosend, dorecv, fsem, frsem,
):
    g = lax.axis_index("group")
    z = lax.axis_index("ctx_0")
    x = lax.axis_index("ctx_1")
    sends = (send0, send1, send2, send3)
    recvs = (recv0, recv1, recv2, recv3)
    nears = (near0, near1, near2, near3)
    cuts = (near0, cut1, cut2, cut3)
    limit = plen[0]
    turn = 1 + 2 * rot(g, 2)
    up_z, down_z = rot(z + 1, ROWS), rot(z + ROWS - 1, ROWS)

    load_q = pltpu.make_async_copy(qraw_any, qraw, lsem.at[COLS + 1])
    load_kv = pltpu.make_async_copy(skv_any, skv, lsem.at[COLS + 2])
    load_pool = pltpu.make_async_copy(pool_any, pool, lsem.at[COLS])
    load_q.start()
    load_kv.start()
    load_pool.start()
    barrier = pltpu.get_barrier_semaphore()
    partners = [(rot(g + n, GROUPS), z, x) for n in range(1, GROUPS)]
    partners += [(g, z, rot(x + n, COLS)) for n in range(1, COLS)]
    partners += [(g, up_z, x), (g, down_z, x)]
    for to in partners:
        pl.semaphore_signal(barrier, inc=1, device_id=to, device_id_type=MESH)

    mix[...] = jnp.full((8, HEAD), -1, jnp.int32)
    mix[0:1, 0:PAGES] = owner[...]
    mix[1:2, 0:PAGES] = slots[...]
    lane = lax.broadcasted_iota(jnp.int32, (HEAD, HEAD), 1)
    line = lax.broadcasted_iota(jnp.int32, (HEAD, HEAD), 0)
    owners = jnp.broadcast_to(mix[0:1, :], (HEAD, HEAD))
    earlier = (owners == owners.T) & (line < lane)
    rank = jnp.sum(jnp.where(earlier, 1, 0), axis=0, keepdims=True)
    place = mix[0:1, :] * CAP + rank
    places = jnp.broadcast_to(place, (HEAD, HEAD)).T
    named = jnp.broadcast_to(mix[1:2, :], (HEAD, HEAD)).T
    wanted = (places == lane) & (line < PAGES)
    tab[0:1, :] = jnp.sum(jnp.where(wanted, named, 0), axis=0, keepdims=True)
    tab[1:2, :] = place
    tab[2:8, :] = jnp.zeros((6, HEAD), jnp.int32)

    token_at = limit + (z * COLS + x) * TOKENS + lax.broadcasted_iota(jnp.int32, (TOKENS, HEAD), 0)
    angles = token_at.astype(F32) * freq[...]
    cosf = jnp.cos(angles)
    sinf = jnp.sin(angles)
    upper = lax.broadcasted_iota(jnp.int32, (TOKENS, HEAD), 1) >= HEAD // 2
    sinf = jnp.where(upper, sinf, -sinf)
    scale = HEAD ** (-0.5) * 1.4426950408889634

    def turned(raw, gain):
        raw = raw.astype(F32)
        mean = jnp.mean(raw * raw, axis=-1, keepdims=True)
        flat = raw * lax.rsqrt(mean + EPS) * gain
        return flat * cosf + pltpu.roll(flat, HEAD // 2, 1) * sinf

    load_q.wait()
    load_kv.wait()
    for i in range(COLS * RATIO):
        part = turned(qraw[:, i * HEAD : (i + 1) * HEAD], qgain[...])
        qsend[i // RATIO, i % RATIO] = (part * scale).astype(BF16)
    for i in range(COLS):
        part = turned(skv[:, i * HEAD : (i + 1) * HEAD], kgain[...])
        qsend[i, RATIO] = part.astype(BF16)
        qsend[i, RATIO + 1] = skv[:, (COLS + i) * HEAD : (COLS + i + 1) * HEAD]

    pl.semaphore_wait(barrier, len(partners))

    def req_copy(d):
        to = rot(g + d, GROUPS)
        return pltpu.make_async_remote_copy(
            src_ref=tab, dst_ref=reqv.at[g], send_sem=rsend.at[d], recv_sem=rrecv.at[d],
            device_id=(to, z, x), device_id_type=MESH,
        )

    mine = z * COLS + x

    def q_copy(k):
        to = rot(x + k, COLS)
        return pltpu.make_async_remote_copy(
            src_ref=qsend.at[to], dst_ref=qbuf.at[mine], send_sem=xsend.at[k], recv_sem=xrecv.at[k],
            device_id=(g, z, to), device_id_type=MESH,
        )

    for d in range(1, GROUPS):
        req_copy(d).start()
    for k in range(1, COLS):
        q_copy(k).start()

    def ring_copy(s, k, up):
        col = rot(x + COLS - k, COLS)
        away = rot(z + ROWS - s, ROWS) if up else rot(z + s, ROWS)
        place = away * COLS + col
        if s == 0 and k == 0:
            src = qsend.at[x, pl.ds(0, RATIO + 1)]
        else:
            src = qbuf.at[place, pl.ds(0, RATIO + 1)]
        return pltpu.make_async_remote_copy(
            src_ref=src, dst_ref=qbuf.at[place, pl.ds(0, RATIO + 1)],
            send_sem=(upsend if up else dnsend).at[s, k],
            recv_sem=(uprecv if up else dnrecv).at[s, k],
            device_id=(g, up_z if up else down_z, x), device_id_type=MESH,
        )

    ring_copy(0, 0, True).start()
    ring_copy(0, 0, False).start()
    qbuf[mine] = qsend[x]

    own_req = pltpu.make_async_copy(tab, reqs.at[g], ssem.at[0])
    own_req.start()

    def req_local(d):
        frm = rot(g + GROUPS - d, GROUPS)
        return pltpu.make_async_copy(reqv.at[frm], reqs.at[frm], ssem.at[d])

    for d in range(1, GROUPS):
        req_copy(d).wait_recv()
        req_local(d).start()
    own_req.wait()
    for d in range(1, GROUPS):
        req_local(d).wait()
    load_pool.wait()

    def page_copy(k, d):
        to = rot(g + d, GROUPS)
        return pltpu.make_async_remote_copy(
            src_ref=sends[k].at[pl.ds(to * CAP, CAP)], dst_ref=recvs[k].at[pl.ds(g * CAP, CAP)],
            send_sem=psend.at[k, d], recv_sem=precv.at[k, d],
            device_id=(to, z, x), device_id_type=MESH,
        )

    def own_pages(k):
        own = pl.ds(g * CAP, CAP)
        return pltpu.make_async_copy(sends[k].at[own], recvs[k].at[own], lsem.at[k])

    def gather(k):
        @pl.loop(0, GROUPS)
        def _(d):
            to = rot(g + d, GROUPS)
            head = rot(x + k * (1 + 2 * rot(to, 2)), COLS)
            key_at = pl.multiple_of(head * HEAD, HEAD)
            value_at = pl.multiple_of((COLS + head) * HEAD, HEAD)
            for r in range(CAP):
                slot = reqs[to, 0, g * CAP + r]
                sends[k][to * CAP + r, :, 0:HEAD] = pool[slot, :, pl.ds(key_at, HEAD)]
                sends[k][to * CAP + r, :, HEAD : 2 * HEAD] = pool[slot, :, pl.ds(value_at, HEAD)]

            @pl.when(d > 0)
            def _():
                page_copy(k, d).start()

        own_pages(k).start()

    for k in (1, 2, 3, 0):
        gather(k)

    def near_copy(k):
        return pltpu.make_async_remote_copy(
            src_ref=cuts[k], dst_ref=nears[k], send_sem=nsend.at[k], recv_sem=nrecv.at[k],
            device_id=(g, z, rot(x + k * turn, COLS)), device_id_type=MESH,
        )

    def compact(k):
        for d in range(1, GROUPS):
            page_copy(k, d).wait_recv()
        own_pages(k).wait()

        @pl.loop(0, PAGES // 4)
        def _(j):
            for i in range(4):
                rows = pl.ds(pl.multiple_of((j * 4 + i) * PAGE, PAGE), PAGE)
                cuts[k][rows, :] = recvs[k][reqs[g, 1, j * 4 + i]]

        if k:
            near_copy(k).start()

    for k in range(1, COLS):
        q_copy(k).wait_recv()
        ring_copy(0, k, True).start()
        ring_copy(0, k, False).start()
    for s in range(1, 5):
        for k in range(COLS):
            if s < 4 or k in FIRST_UP:
                ring_copy(s - 1, k, True).wait_recv()
            if s < 3 or (s == 3 and k in FIRST_UP):
                ring_copy(s, k, True).start()
            if s < 4 or k in FIRST_DOWN:
                ring_copy(s - 1, k, False).wait_recv()
            if s < 3 or (s == 3 and k in FIRST_DOWN):
                ring_copy(s, k, False).start()
        if s == 2:
            compact(1)

    def queries(zb, c):
        part = qbuf[pl.ds(zb * COLS + 2 * c, 2), 0:RATIO]
        return part.reshape(HALF, HEAD)

    for b in range(COLS):
        rows = slice(KEYS + b * TOKENS, KEYS + (b + 1) * TOKENS)
        kc[rows, :] = qbuf[z * COLS + b, RATIO]
    kc[KEYS + COLS * TOKENS :, :] = jnp.zeros((HEAD - COLS * TOKENS, HEAD), BF16)
    suffix_v = [qbuf[z * COLS + b, RATIO + 1].astype(F32) for b in range(COLS)]
    suffix_v = jnp.concatenate(suffix_v + [jnp.zeros((HEAD - COLS * TOKENS, HEAD), F32)], axis=0)
    vt[0:HEAD, KEYS:] = suffix_v.T.astype(BF16)
    vt[HEAD:, KEYS:] = jnp.ones((SUMROWS, HEAD), BF16)

    shared_key = qbuf[0, RATIO][0:1, :].astype(F32)

    def prepare(k):
        base = (z * COLS + rot(x + 3 * COLS - k * turn, COLS)) * KEYS
        for b in range(KEYS // HEAD):
            rows = slice(b * HEAD, (b + 1) * HEAD)
            token = base + b * HEAD + lax.broadcasted_iota(jnp.int32, (HEAD, HEAD), 0)
            seen = token < limit
            keys = nears[k][rows, 0:HEAD].astype(F32)
            values = nears[k][rows, HEAD:].astype(F32)
            kc[rows, :] = jnp.where(seen, keys, shared_key).astype(BF16)
            vt[0:HEAD, rows] = jnp.where(seen, values, 0.0).T.astype(BF16)
        lane = base + lax.broadcasted_iota(jnp.int32, (SUMROWS, KEYS), 1)
        vt[HEAD:, 0:KEYS] = jnp.where(lane < limit, 1.0, 0.0).astype(BF16)

    def scores(dst, peak, zb, c, first):
        step(None, None, 0, 0, dst, peak, zb, c, first)

    def finish(src, peak, zb, c, first):
        step(src, peak, zb, c, None, None, 0, 0, first)

    def step(src, src_peak, zb, c, dst, dst_peak, next_zb, next_c, first):
        size = WIDE if first else KEYS
        if src is not None:
            top = src_peak[0:1, :]
            if not first:
                before = jnp.concatenate([mref[zb, q, 0:1, :] for q in (2 * c, 2 * c + 1)], axis=1)
                top = jnp.maximum(before, top)
        if dst is not None:
            asked = queries(next_zb, next_c)
        weights, tops = [], []
        for lo in range(0, size, CUT):
            hi = min(lo + CUT, size)
            if dst is not None:
                s = lax.dot_general(
                    kc[lo:hi, :], asked, (((1,), (1,)), ((), ())), preferred_element_type=F32
                )
                if hi > KEYS:
                    key_row = lax.broadcasted_iota(jnp.int32, (hi - lo, HALF), 0) + (lo - KEYS)
                    column = lax.broadcasted_iota(jnp.int32, (hi - lo, HALF), 1)
                    asker = next_zb * (COLS * TOKENS) + (column // HEAD + 2 * next_c) * TOKENS
                    asker = asker + (column & (TOKENS - 1))
                    seen = (key_row < COLS * TOKENS) & (z * (COLS * TOKENS) + key_row <= asker)
                    s = jnp.where((key_row < 0) | seen, s, FLOOR)
                dst[lo:hi, :] = s
                tops.append(jnp.max(s, axis=0, keepdims=True))
            if src is not None:
                weights.append(jnp.exp2(src[lo:hi, :] - top).astype(BF16))
        if dst is not None:
            best = tops[0]
            for t in tops[1:]:
                best = jnp.maximum(best, t)
            dst_peak[0:1, :] = jnp.ceil(best * 0.25) * 4.0
        if src is not None:
            fresh = jnp.dot(vt[:, 0:size], jnp.concatenate(weights, axis=0), preferred_element_type=F32)
            for i in range(2):
                q, at = 2 * c + i, slice(i * HEAD, (i + 1) * HEAD)
                part = fresh[:, at]
                if not first:
                    part = oacc[zb, q] * jnp.exp2(before[:, at] - top[:, at]) + part
                oacc[zb, q] = part
                mref[zb, q, 0:1, :] = top[:, at]

    def attend(k, first):
        if k:
            near_copy(k).wait_recv()
        prepare(k)
        scores(sa, pa, 0, 0, first)

        @pl.loop(0, ROWS)
        def _(zb):
            step(sa, pa, zb, 0, sb, pb, zb, 1, first)
            step(sb, pb, zb, 1, sa, pa, jnp.minimum(zb + 1, ROWS - 1), 0, first)

    def quarter(j):
        return rot(x + QUARTERS[j], COLS)

    def sum_copy(s, j, up):
        block = rot(z + 4 - s, ROWS) if up else rot(z + 4 + s, ROWS)
        return pltpu.make_async_remote_copy(
            src_ref=osend.at[block, quarter(j)], dst_ref=(upin if up else dnin).at[s, j],
            send_sem=(uosend if up else dosend).at[s, j],
            recv_sem=(uorecv if up else dorecv).at[s, j],
            device_id=(g, up_z if up else down_z, x), device_id_type=MESH,
        )

    def own_part(zb, q):
        return oacc[zb, q, 0:HEAD, :], mref[zb, q, 0:1, :], oacc[zb, q, HEAD : HEAD + 1, :]

    def join(part, arrived):
        o, m, l = part
        tile = arrived[HEAD:, :].astype(F32)
        m_in = tile[0:1]
        l_in = tile[1:2] + tile[2:3]
        top = jnp.maximum(m, m_in)
        mul, mul_in = jnp.exp2(m - top), jnp.exp2(m_in - top)
        return o * mul + arrived[0:HEAD, :].astype(F32) * mul_in, top, l * mul + l_in * mul_in

    def pack(zb, q, part):
        o, m, l = part
        l_high = l.astype(BF16).astype(F32)
        row = lax.broadcasted_iota(jnp.int32, (SUMROWS, HEAD), 0)
        tile = jnp.where(row == 0, m, jnp.where(row == 1, l_high, jnp.where(row == 2, l - l_high, 0.0)))
        osend[zb, q, 0:HEAD, :] = o.astype(BF16)
        osend[zb, q, HEAD:, :] = tile.astype(BF16)

    def relay(s, early, late):
        for js in zip(early, late):
            for up, j in zip((True, False), js):
                block = rot(z + 4 - s, ROWS) if up else rot(z + 4 + s, ROWS)
                q = quarter(j)
                part = own_part(block, q)
                if s > 1 or (s == 1 and j in (FIRST_UP if up else FIRST_DOWN)):
                    sum_copy(s - 1, j, up).wait_recv()
                    part = join(part, (upin if up else dnin).at[s - 1, j])
                pack(block, q, part)
                sum_copy(s, j, up).start()

    def f_copy(q, k):
        return pltpu.make_async_remote_copy(
            src_ref=fsend.at[q], dst_ref=frecv.at[x], send_sem=fsem.at[k], recv_sem=frsem.at[k],
            device_id=(g, z, q), device_id_type=MESH,
        )

    compact(2)
    attend(1, True)
    compact(3)
    attend(2, False)
    attend(3, False)
    compact(0)
    prepare(0)

    def block_at(n):
        return rot(z + LAST[n], ROWS)

    scores(sa, pa, block_at(0), 0, False)
    for n in range(ROWS):
        step(sa, pa, block_at(n), 0, sb, pb, block_at(n), 1, False)
        if n < ROWS - 1:
            step(sb, pb, block_at(n), 1, sa, pa, block_at(n + 1), 0, False)
        else:
            finish(sb, pb, block_at(n), 1, False)
        if n == 0:
            relay(0, FIRST_UP, FIRST_DOWN)
        if n == 2:
            relay(1, FIRST_DOWN, FIRST_UP)
        if n == 4:
            relay(1, FIRST_UP, FIRST_DOWN)
        if n == 6:
            relay(2, FIRST_DOWN, FIRST_UP)
    relay(2, FIRST_UP, FIRST_DOWN)
    relay(3, FIRST_DOWN, FIRST_UP)
    relay(3, FIRST_UP, FIRST_DOWN)

    for j in range(COLS):
        q = quarter(j)
        part = own_part(z, q)
        sum_copy(3, j, False).wait_recv()
        part = join(part, dnin.at[3, j])
        sum_copy(3, j, True).wait_recv()
        o, m, l = join(part, upin.at[3, j])
        fsend[q] = (o / l).T.astype(BF16).reshape(RATIO, TOKENS, HEAD)
        if QUARTERS[j]:
            f_copy(q, QUARTERS[j]).start()

    frecv[x] = fsend[x]
    for k in range(1, COLS):
        f_copy(rot(x + k, COLS), k).wait_recv()
    for h in range(COLS):
        for i in range(RATIO):
            at = (h * RATIO + i) * HEAD
            out[:, at : at + HEAD] = frecv[h, i].astype(F32)

    for d in range(1, GROUPS):
        req_copy(d).wait_send()
    for k in range(1, COLS):
        q_copy(k).wait_send()
        near_copy(k).wait_send()
        f_copy(rot(x + k, COLS), k).wait_send()
    for s in range(4):
        for k in range(COLS):
            if s < 3 or k in FIRST_UP:
                ring_copy(s, k, True).wait_send()
            if s < 3 or k in FIRST_DOWN:
                ring_copy(s, k, False).wait_send()
            if s or k in FIRST_UP:
                sum_copy(s, k, True).wait_send()
            if s or k in FIRST_DOWN:
                sum_copy(s, k, False).wait_send()
    for k in range(COLS):
        for d in range(1, GROUPS):
            page_copy(k, d).wait_send()


def shards(
    query_raw, suffix_keyval, query_gain, key_norm_gain, positions, prefix_length,
    page_owner, page_slot, cache_pool,
):
    half = np.arange(HEAD) % (HEAD // 2)
    frequency = (1000000.0 ** (-(2.0 / HEAD) * half)).astype(np.float32)[None]
    vmem = pl.BlockSpec(memory_space=pltpu.VMEM)
    far = pl.BlockSpec(memory_space=pl.ANY)
    page_half = (GROUPS * CAP, PAGE, 2 * HEAD)
    dma = pltpu.SemaphoreType.DMA
    result = pl.pallas_call(
        kernel,
        out_shape=jax.ShapeDtypeStruct((TOKENS, COLS * RATIO * HEAD), F32),
        in_specs=[vmem] * 3 + [far] * 2 + [vmem] * 2 + [pl.BlockSpec(memory_space=pltpu.SMEM), far],
        out_specs=vmem,
        scratch_shapes=[
            pltpu.VMEM((TOKENS, COLS * RATIO * HEAD), BF16),
            pltpu.VMEM((TOKENS, 2 * COLS * HEAD), BF16),
            pltpu.VMEM((8, HEAD), jnp.int32),
            pltpu.VMEM((8, HEAD), jnp.int32),
        ]
        + [pltpu.VMEM((POOL, PAGE, 2 * COLS * HEAD), BF16)]
        + [pltpu.VMEM(page_half, BF16)] * 8
        + [pltpu.VMEM((KEYS, 2 * HEAD), BF16)] * 7
        + [
            pltpu.VMEM((WIDE, HEAD), BF16),
            pltpu.VMEM((HEAD + SUMROWS, WIDE), BF16),
            pltpu.VMEM((WIDE, HALF), F32),
            pltpu.VMEM((WIDE, HALF), F32),
            pltpu.VMEM((8, HALF), F32),
            pltpu.VMEM((8, HALF), F32),
            pltpu.VMEM((COLS, RATIO + 2, TOKENS, HEAD), BF16),
            pltpu.VMEM((ROWS * COLS, RATIO + 2, TOKENS, HEAD), BF16),
            pltpu.VMEM((ROWS, COLS, HEAD + SUMROWS, HEAD), F32),
            pltpu.VMEM((ROWS, COLS, 8, HEAD), F32),
            pltpu.VMEM((ROWS, COLS, HEAD + SUMROWS, HEAD), BF16),
            pltpu.VMEM((4, COLS, HEAD + SUMROWS, HEAD), BF16),
            pltpu.VMEM((4, COLS, HEAD + SUMROWS, HEAD), BF16),
            pltpu.VMEM((COLS, RATIO, TOKENS, HEAD), BF16),
            pltpu.VMEM((COLS, RATIO, TOKENS, HEAD), BF16),
            pltpu.VMEM((GROUPS, 8, HEAD), jnp.int32),
            pltpu.SMEM((GROUPS, 8, HEAD), jnp.int32),
            dma((COLS, GROUPS)), dma((COLS, GROUPS)), dma((COLS + 3,)),
            dma((GROUPS,)), dma((GROUPS,)), dma((GROUPS,)),
            dma((COLS,)), dma((COLS,)),
            dma((4, COLS)), dma((4, COLS)), dma((4, COLS)), dma((4, COLS)),
            dma((COLS,)), dma((COLS,)),
            dma((4, COLS)), dma((4, COLS)), dma((4, COLS)), dma((4, COLS)),
            dma((COLS,)), dma((COLS,)),
        ],
        compiler_params=pltpu.CompilerParams(
            collective_id=0, has_side_effects=True, vmem_limit_bytes=60 * 1024 * 1024
        ),
        name="spanned",
    )(
        page_owner.reshape(1, PAGES), page_slot, jnp.asarray(frequency), query_raw[0],
        suffix_keyval[0], query_gain[None], key_norm_gain[None], prefix_length, cache_pool[0],
    )
    return result.astype(BF16)[None]


def solution(mesh):
    finer = Mesh(mesh.devices.reshape(GROUPS, ROWS, COLS), ("group", "ctx_0", "ctx_1"))
    ctx = ("ctx_0", "ctx_1")
    in_specs = (
        P("group", ctx, None),
        P("group", ctx, None),
        P(),
        P(),
        P("group", ctx),
        P("group"),
        P("group", ctx, None),
        P("group", ctx),
        P("group", ctx, None, None),
    )
    return jax.shard_map(
        shards, mesh=finer, in_specs=in_specs, out_specs=P("group", ctx, None), check_vma=False
    )
```

```python
import jax
import jax.numpy as jnp
import numpy as np
from jax import lax
from jax.experimental import pallas as pl
from jax.experimental.pallas import tpu as pltpu
from jax.sharding import Mesh
from jax.sharding import PartitionSpec as P

MESH = pl.DeviceIdType.MESH
EPS = 1e-06
FLOOR = -65536.0
GROUPS = 8
ROWS = 8
COLS = 4
CAP = 12
PAGES = 48
POOL = 96
PAGE = 16
HEAD = 128
TOKENS = 16
RATIO = 8
KEYS = PAGES * PAGE
BLOCK = COLS * RATIO * TOKENS
HALF = BLOCK // 2
SUMROWS = 8
WIDE = KEYS + HEAD
CUT = 384
LAST = (4, 3, 5, 2, 6, 1, 7, 0)
QUARTERS = (2, 1, 3, 0)
FIRST_UP = (0, 1)
FIRST_DOWN = (2, 3)
F32 = jnp.float32
BF16 = jnp.bfloat16


def rot(a, n):
    return lax.rem(a, jnp.int32(n))


def kernel(
    owner, slots, freq, qraw_any, skv_any, qgain, kgain, plen, pool_any, out,
    qraw, skv, mix, tab, pool, send0, send1, send2, send3, recv0, recv1, recv2, recv3,
    near0, near1, near2, near3, cut1, cut2, cut3,
    kc, vt, sa, sb, pa, pb, qsend, qbuf, oacc, mref, osend, upin, dnin, upend, dnend, ownend,
    reqv, reqs,
    psend, precv, lsem, rsend, rrecv, ssem, xsend, xrecv,
    upsend, uprecv, dnsend, dnrecv, nsend, nrecv, uosend, uorecv, dosend, dorecv, fsem, frsem,
):
    g = lax.axis_index("group")
    z = lax.axis_index("ctx_0")
    x = lax.axis_index("ctx_1")
    sends = (send0, send1, send2, send3)
    recvs = (recv0, recv1, recv2, recv3)
    nears = (near0, near1, near2, near3)
    cuts = (near0, cut1, cut2, cut3)
    limit = plen[0]
    turn = 1 + 2 * rot(g, 2)
    up_z, down_z = rot(z + 1, ROWS), rot(z + ROWS - 1, ROWS)

    load_q = pltpu.make_async_copy(qraw_any, qraw, lsem.at[COLS + 1])
    load_kv = pltpu.make_async_copy(skv_any, skv, lsem.at[COLS + 2])
    load_pool = pltpu.make_async_copy(pool_any, pool, lsem.at[COLS])
    load_q.start()
    load_kv.start()
    load_pool.start()
    barrier = pltpu.get_barrier_semaphore()
    partners = [(rot(g + n, GROUPS), z, x) for n in range(1, GROUPS)]
    partners += [(g, z, rot(x + n, COLS)) for n in range(1, COLS)]
    partners += [(g, to_z, rot(x + n, COLS)) for n in range(COLS) for to_z in (up_z, down_z)]
    for to in partners:
        pl.semaphore_signal(barrier, inc=1, device_id=to, device_id_type=MESH)

    mix[...] = jnp.full((8, HEAD), -1, jnp.int32)
    mix[0:1, 0:PAGES] = owner[...]
    mix[1:2, 0:PAGES] = slots[...]
    lane = lax.broadcasted_iota(jnp.int32, (HEAD, HEAD), 1)
    line = lax.broadcasted_iota(jnp.int32, (HEAD, HEAD), 0)
    owners = jnp.broadcast_to(mix[0:1, :], (HEAD, HEAD))
    earlier = (owners == owners.T) & (line < lane)
    rank = jnp.sum(jnp.where(earlier, 1, 0), axis=0, keepdims=True)
    place = mix[0:1, :] * CAP + rank
    places = jnp.broadcast_to(place, (HEAD, HEAD)).T
    named = jnp.broadcast_to(mix[1:2, :], (HEAD, HEAD)).T
    wanted = (places == lane) & (line < PAGES)
    tab[0:1, :] = jnp.sum(jnp.where(wanted, named, 0), axis=0, keepdims=True)
    tab[1:2, :] = place
    tab[2:8, :] = jnp.zeros((6, HEAD), jnp.int32)

    token_at = limit + (z * COLS + x) * TOKENS + lax.broadcasted_iota(jnp.int32, (TOKENS, HEAD), 0)
    angles = token_at.astype(F32) * freq[...]
    cosf = jnp.cos(angles)
    sinf = jnp.sin(angles)
    upper = lax.broadcasted_iota(jnp.int32, (TOKENS, HEAD), 1) >= HEAD // 2
    sinf = jnp.where(upper, sinf, -sinf)
    scale = HEAD ** (-0.5) * 1.4426950408889634

    def turned(raw, gain):
        raw = raw.astype(F32)
        mean = jnp.mean(raw * raw, axis=-1, keepdims=True)
        flat = raw * lax.rsqrt(mean + EPS) * gain
        return flat * cosf + pltpu.roll(flat, HEAD // 2, 1) * sinf

    load_q.wait()
    load_kv.wait()
    for i in range(COLS * RATIO):
        part = turned(qraw[:, i * HEAD : (i + 1) * HEAD], qgain[...])
        qsend[i // RATIO, i % RATIO] = (part * scale).astype(BF16)
    for i in range(COLS):
        part = turned(skv[:, i * HEAD : (i + 1) * HEAD], kgain[...])
        qsend[i, RATIO] = part.astype(BF16)
        qsend[i, RATIO + 1] = skv[:, (COLS + i) * HEAD : (COLS + i + 1) * HEAD]

    pl.semaphore_wait(barrier, len(partners))

    def req_copy(d):
        to = rot(g + d, GROUPS)
        return pltpu.make_async_remote_copy(
            src_ref=tab, dst_ref=reqv.at[g], send_sem=rsend.at[d], recv_sem=rrecv.at[d],
            device_id=(to, z, x), device_id_type=MESH,
        )

    mine = z * COLS + x

    def q_copy(k):
        to = rot(x + k, COLS)
        return pltpu.make_async_remote_copy(
            src_ref=qsend.at[to], dst_ref=qbuf.at[mine], send_sem=xsend.at[k], recv_sem=xrecv.at[k],
            device_id=(g, z, to), device_id_type=MESH,
        )

    for d in range(1, GROUPS):
        req_copy(d).start()
    for k in range(1, COLS):
        q_copy(k).start()

    def ring_copy(s, k, up):
        col = rot(x + COLS - k, COLS)
        away = rot(z + ROWS - s, ROWS) if up else rot(z + s, ROWS)
        place = away * COLS + col
        if s == 0 and k == 0:
            src = qsend.at[x, pl.ds(0, RATIO + 1)]
        else:
            src = qbuf.at[place, pl.ds(0, RATIO + 1)]
        return pltpu.make_async_remote_copy(
            src_ref=src, dst_ref=qbuf.at[place, pl.ds(0, RATIO + 1)],
            send_sem=(upsend if up else dnsend).at[s, k],
            recv_sem=(uprecv if up else dnrecv).at[s, k],
            device_id=(g, up_z if up else down_z, x), device_id_type=MESH,
        )

    ring_copy(0, 0, True).start()
    ring_copy(0, 0, False).start()
    qbuf[mine] = qsend[x]

    own_req = pltpu.make_async_copy(tab, reqs.at[g], ssem.at[0])
    own_req.start()

    def req_local(d):
        frm = rot(g + GROUPS - d, GROUPS)
        return pltpu.make_async_copy(reqv.at[frm], reqs.at[frm], ssem.at[d])

    for d in range(1, GROUPS):
        req_copy(d).wait_recv()
        req_local(d).start()
    own_req.wait()
    for d in range(1, GROUPS):
        req_local(d).wait()
    load_pool.wait()

    def page_copy(k, d):
        to = rot(g + d, GROUPS)
        return pltpu.make_async_remote_copy(
            src_ref=sends[k].at[pl.ds(to * CAP, CAP)], dst_ref=recvs[k].at[pl.ds(g * CAP, CAP)],
            send_sem=psend.at[k, d], recv_sem=precv.at[k, d],
            device_id=(to, z, x), device_id_type=MESH,
        )

    def own_pages(k):
        own = pl.ds(g * CAP, CAP)
        return pltpu.make_async_copy(sends[k].at[own], recvs[k].at[own], lsem.at[k])

    def gather(k):
        @pl.loop(0, GROUPS)
        def _(d):
            to = rot(g + d, GROUPS)
            head = rot(x + k * (1 + 2 * rot(to, 2)), COLS)
            key_at = pl.multiple_of(head * HEAD, HEAD)
            value_at = pl.multiple_of((COLS + head) * HEAD, HEAD)
            for r in range(CAP):
                slot = reqs[to, 0, g * CAP + r]
                sends[k][to * CAP + r, :, 0:HEAD] = pool[slot, :, pl.ds(key_at, HEAD)]
                sends[k][to * CAP + r, :, HEAD : 2 * HEAD] = pool[slot, :, pl.ds(value_at, HEAD)]

            @pl.when(d > 0)
            def _():
                page_copy(k, d).start()

        own_pages(k).start()

    for k in (1, 2, 3, 0):
        gather(k)

    def near_copy(k):
        return pltpu.make_async_remote_copy(
            src_ref=cuts[k], dst_ref=nears[k], send_sem=nsend.at[k], recv_sem=nrecv.at[k],
            device_id=(g, z, rot(x + k * turn, COLS)), device_id_type=MESH,
        )

    def compact(k):
        for d in range(1, GROUPS):
            page_copy(k, d).wait_recv()
        own_pages(k).wait()

        @pl.loop(0, PAGES // 4)
        def _(j):
            for i in range(4):
                rows = pl.ds(pl.multiple_of((j * 4 + i) * PAGE, PAGE), PAGE)
                cuts[k][rows, :] = recvs[k][reqs[g, 1, j * 4 + i]]

        if k:
            near_copy(k).start()

    for k in range(1, COLS):
        q_copy(k).wait_recv()
        ring_copy(0, k, True).start()
        ring_copy(0, k, False).start()
    for s in range(1, 5):
        for k in range(COLS):
            if s < 4 or k in FIRST_UP:
                ring_copy(s - 1, k, True).wait_recv()
            if s < 3 or (s == 3 and k in FIRST_UP):
                ring_copy(s, k, True).start()
            if s < 4 or k in FIRST_DOWN:
                ring_copy(s - 1, k, False).wait_recv()
            if s < 3 or (s == 3 and k in FIRST_DOWN):
                ring_copy(s, k, False).start()
        if s == 2:
            compact(1)

    def queries(zb, c):
        part = qbuf[pl.ds(zb * COLS + 2 * c, 2), 0:RATIO]
        return part.reshape(HALF, HEAD)

    for b in range(COLS):
        rows = slice(KEYS + b * TOKENS, KEYS + (b + 1) * TOKENS)
        kc[rows, :] = qbuf[z * COLS + b, RATIO]
    kc[KEYS + COLS * TOKENS :, :] = jnp.zeros((HEAD - COLS * TOKENS, HEAD), BF16)
    suffix_v = [qbuf[z * COLS + b, RATIO + 1].astype(F32) for b in range(COLS)]
    suffix_v = jnp.concatenate(suffix_v + [jnp.zeros((HEAD - COLS * TOKENS, HEAD), F32)], axis=0)
    vt[0:HEAD, KEYS:] = suffix_v.T.astype(BF16)
    vt[HEAD:, KEYS:] = jnp.ones((SUMROWS, HEAD), BF16)

    shared_key = qbuf[0, RATIO][0:1, :].astype(F32)

    def prepare(k):
        base = (z * COLS + rot(x + 3 * COLS - k * turn, COLS)) * KEYS
        for b in range(KEYS // HEAD):
            rows = slice(b * HEAD, (b + 1) * HEAD)
            token = base + b * HEAD + lax.broadcasted_iota(jnp.int32, (HEAD, HEAD), 0)
            seen = token < limit
            keys = nears[k][rows, 0:HEAD].astype(F32)
            values = nears[k][rows, HEAD:].astype(F32)
            kc[rows, :] = jnp.where(seen, keys, shared_key).astype(BF16)
            vt[0:HEAD, rows] = jnp.where(seen, values, 0.0).T.astype(BF16)
        lane = base + lax.broadcasted_iota(jnp.int32, (SUMROWS, KEYS), 1)
        vt[HEAD:, 0:KEYS] = jnp.where(lane < limit, 1.0, 0.0).astype(BF16)

    def scores(dst, peak, zb, c, first):
        step(None, None, 0, 0, dst, peak, zb, c, first)

    def finish(src, peak, zb, c, first):
        step(src, peak, zb, c, None, None, 0, 0, first)

    def step(src, src_peak, zb, c, dst, dst_peak, next_zb, next_c, first):
        size = WIDE if first else KEYS
        if src is not None:
            top = src_peak[0:1, :]
            if not first:
                before = jnp.concatenate([mref[zb, q, 0:1, :] for q in (2 * c, 2 * c + 1)], axis=1)
                top = jnp.maximum(before, top)
        if dst is not None:
            asked = queries(next_zb, next_c)
        weights, tops = [], []
        for lo in range(0, size, CUT):
            hi = min(lo + CUT, size)
            if dst is not None:
                s = lax.dot_general(
                    kc[lo:hi, :], asked, (((1,), (1,)), ((), ())), preferred_element_type=F32
                )
                if hi > KEYS:
                    key_row = lax.broadcasted_iota(jnp.int32, (hi - lo, HALF), 0) + (lo - KEYS)
                    column = lax.broadcasted_iota(jnp.int32, (hi - lo, HALF), 1)
                    asker = next_zb * (COLS * TOKENS) + (column // HEAD + 2 * next_c) * TOKENS
                    asker = asker + (column & (TOKENS - 1))
                    seen = (key_row < COLS * TOKENS) & (z * (COLS * TOKENS) + key_row <= asker)
                    s = jnp.where((key_row < 0) | seen, s, FLOOR)
                dst[lo:hi, :] = s
                tops.append(jnp.max(s, axis=0, keepdims=True))
            if src is not None:
                weights.append(jnp.exp2(src[lo:hi, :] - top).astype(BF16))
        if dst is not None:
            best = tops[0]
            for t in tops[1:]:
                best = jnp.maximum(best, t)
            dst_peak[0:1, :] = jnp.ceil(best * 0.25) * 4.0
        if src is not None:
            fresh = jnp.dot(vt[:, 0:size], jnp.concatenate(weights, axis=0), preferred_element_type=F32)
            for i in range(2):
                q, at = 2 * c + i, slice(i * HEAD, (i + 1) * HEAD)
                part = fresh[:, at]
                if not first:
                    part = oacc[zb, q] * jnp.exp2(before[:, at] - top[:, at]) + part
                oacc[zb, q] = part
                mref[zb, q, 0:1, :] = top[:, at]

    def attend(k, first):
        if k:
            near_copy(k).wait_recv()
        prepare(k)
        scores(sa, pa, 0, 0, first)

        @pl.loop(0, ROWS)
        def _(zb):
            step(sa, pa, zb, 0, sb, pb, zb, 1, first)
            step(sb, pb, zb, 1, sa, pa, jnp.minimum(zb + 1, ROWS - 1), 0, first)

    def quarter(j):
        return rot(x + QUARTERS[j], COLS)

    def sum_copy(s, j, up):
        block = rot(z + 4 - s, ROWS) if up else rot(z + 4 + s, ROWS)
        if s < 3:
            dst, to_x = (upin if up else dnin).at[s, j], x
        else:
            dst, to_x = (upend if up else dnend).at[x], quarter(j)
        return pltpu.make_async_remote_copy(
            src_ref=osend.at[block, quarter(j)], dst_ref=dst,
            send_sem=(uosend if up else dosend).at[s, j],
            recv_sem=(uorecv if up else dorecv).at[s, j],
            device_id=(g, up_z if up else down_z, to_x), device_id_type=MESH,
        )

    def own_copy(j):
        return pltpu.make_async_remote_copy(
            src_ref=osend.at[z, quarter(j)], dst_ref=ownend.at[x],
            send_sem=fsem.at[j], recv_sem=frsem.at[j],
            device_id=(g, z, quarter(j)), device_id_type=MESH,
        )

    def own_part(zb, q):
        return oacc[zb, q, 0:HEAD, :], mref[zb, q, 0:1, :], oacc[zb, q, HEAD : HEAD + 1, :]

    def join(part, arrived):
        o, m, l = part
        tile = arrived[HEAD:, :].astype(F32)
        m_in = tile[0:1]
        l_in = tile[1:2] + tile[2:3]
        top = jnp.maximum(m, m_in)
        mul, mul_in = jnp.exp2(m - top), jnp.exp2(m_in - top)
        return o * mul + arrived[0:HEAD, :].astype(F32) * mul_in, top, l * mul + l_in * mul_in

    def pack(zb, q, part):
        o, m, l = part
        l_high = l.astype(BF16).astype(F32)
        row = lax.broadcasted_iota(jnp.int32, (SUMROWS, HEAD), 0)
        tile = jnp.where(row == 0, m, jnp.where(row == 1, l_high, jnp.where(row == 2, l - l_high, 0.0)))
        osend[zb, q, 0:HEAD, :] = o.astype(BF16)
        osend[zb, q, HEAD:, :] = tile.astype(BF16)

    def relay(s, early, late):
        for js in zip(early, late):
            for up, j in zip((True, False), js):
                block = rot(z + 4 - s, ROWS) if up else rot(z + 4 + s, ROWS)
                q = quarter(j)
                part = own_part(block, q)
                if s > 1 or (s == 1 and j in (FIRST_UP if up else FIRST_DOWN)):
                    sum_copy(s - 1, j, up).wait_recv()
                    part = join(part, (upin if up else dnin).at[s - 1, j])
                pack(block, q, part)
                sum_copy(s, j, up).start()

    compact(2)
    attend(1, True)
    compact(3)
    attend(2, False)
    attend(3, False)
    compact(0)
    prepare(0)

    def block_at(n):
        return rot(z + LAST[n], ROWS)

    scores(sa, pa, block_at(0), 0, False)
    for n in range(ROWS):
        step(sa, pa, block_at(n), 0, sb, pb, block_at(n), 1, False)
        if n < ROWS - 1:
            step(sb, pb, block_at(n), 1, sa, pa, block_at(n + 1), 0, False)
        else:
            finish(sb, pb, block_at(n), 1, False)
        if n == 0:
            relay(0, FIRST_UP, FIRST_DOWN)
        if n == 2:
            relay(1, FIRST_DOWN, FIRST_UP)
        if n == 4:
            relay(1, FIRST_UP, FIRST_DOWN)
        if n == 6:
            relay(2, FIRST_DOWN, FIRST_UP)
    for j in range(COLS):
        pack(z, quarter(j), own_part(z, quarter(j)))
        if QUARTERS[j]:
            own_copy(j).start()
    ownend[x] = osend[z, x]
    relay(2, FIRST_UP, FIRST_DOWN)
    relay(3, FIRST_DOWN, FIRST_UP)
    relay(3, FIRST_UP, FIRST_DOWN)

    for j in range(COLS):
        if QUARTERS[j]:
            own_copy(j).wait_recv()
        sum_copy(3, j, False).wait_recv()
        sum_copy(3, j, True).wait_recv()
    for h in range(COLS):
        tile = ownend[h, HEAD:, :].astype(F32)
        part = (ownend[h, 0:HEAD, :].astype(F32), tile[0:1], tile[1:2] + tile[2:3])
        o, m, l = join(join(part, dnend.at[h]), upend.at[h])
        rows = (o / l).T.astype(BF16).astype(F32)
        for i in range(RATIO):
            at = (h * RATIO + i) * HEAD
            out[:, at : at + HEAD] = rows[i * TOKENS : (i + 1) * TOKENS]

    for d in range(1, GROUPS):
        req_copy(d).wait_send()
    for k in range(1, COLS):
        q_copy(k).wait_send()
        near_copy(k).wait_send()
        own_copy(k - 1).wait_send()
    for s in range(4):
        for k in range(COLS):
            if s < 3 or k in FIRST_UP:
                ring_copy(s, k, True).wait_send()
            if s < 3 or k in FIRST_DOWN:
                ring_copy(s, k, False).wait_send()
            if s or k in FIRST_UP:
                sum_copy(s, k, True).wait_send()
            if s or k in FIRST_DOWN:
                sum_copy(s, k, False).wait_send()
    for k in range(COLS):
        for d in range(1, GROUPS):
            page_copy(k, d).wait_send()


def shards(
    query_raw, suffix_keyval, query_gain, key_norm_gain, positions, prefix_length,
    page_owner, page_slot, cache_pool,
):
    half = np.arange(HEAD) % (HEAD // 2)
    frequency = (1000000.0 ** (-(2.0 / HEAD) * half)).astype(np.float32)[None]
    vmem = pl.BlockSpec(memory_space=pltpu.VMEM)
    far = pl.BlockSpec(memory_space=pl.ANY)
    page_half = (GROUPS * CAP, PAGE, 2 * HEAD)
    dma = pltpu.SemaphoreType.DMA
    result = pl.pallas_call(
        kernel,
        out_shape=jax.ShapeDtypeStruct((TOKENS, COLS * RATIO * HEAD), F32),
        in_specs=[vmem] * 3 + [far] * 2 + [vmem] * 2 + [pl.BlockSpec(memory_space=pltpu.SMEM), far],
        out_specs=vmem,
        scratch_shapes=[
            pltpu.VMEM((TOKENS, COLS * RATIO * HEAD), BF16),
            pltpu.VMEM((TOKENS, 2 * COLS * HEAD), BF16),
            pltpu.VMEM((8, HEAD), jnp.int32),
            pltpu.VMEM((8, HEAD), jnp.int32),
        ]
        + [pltpu.VMEM((POOL, PAGE, 2 * COLS * HEAD), BF16)]
        + [pltpu.VMEM(page_half, BF16)] * 8
        + [pltpu.VMEM((KEYS, 2 * HEAD), BF16)] * 7
        + [
            pltpu.VMEM((WIDE, HEAD), BF16),
            pltpu.VMEM((HEAD + SUMROWS, WIDE), BF16),
            pltpu.VMEM((WIDE, HALF), F32),
            pltpu.VMEM((WIDE, HALF), F32),
            pltpu.VMEM((8, HALF), F32),
            pltpu.VMEM((8, HALF), F32),
            pltpu.VMEM((COLS, RATIO + 2, TOKENS, HEAD), BF16),
            pltpu.VMEM((ROWS * COLS, RATIO + 2, TOKENS, HEAD), BF16),
            pltpu.VMEM((ROWS, COLS, HEAD + SUMROWS, HEAD), F32),
            pltpu.VMEM((ROWS, COLS, 8, HEAD), F32),
            pltpu.VMEM((ROWS, COLS, HEAD + SUMROWS, HEAD), BF16),
            pltpu.VMEM((3, COLS, HEAD + SUMROWS, HEAD), BF16),
            pltpu.VMEM((3, COLS, HEAD + SUMROWS, HEAD), BF16),
            pltpu.VMEM((COLS, HEAD + SUMROWS, HEAD), BF16),
            pltpu.VMEM((COLS, HEAD + SUMROWS, HEAD), BF16),
            pltpu.VMEM((COLS, HEAD + SUMROWS, HEAD), BF16),
            pltpu.VMEM((GROUPS, 8, HEAD), jnp.int32),
            pltpu.SMEM((GROUPS, 8, HEAD), jnp.int32),
            dma((COLS, GROUPS)), dma((COLS, GROUPS)), dma((COLS + 3,)),
            dma((GROUPS,)), dma((GROUPS,)), dma((GROUPS,)),
            dma((COLS,)), dma((COLS,)),
            dma((4, COLS)), dma((4, COLS)), dma((4, COLS)), dma((4, COLS)),
            dma((COLS,)), dma((COLS,)),
            dma((4, COLS)), dma((4, COLS)), dma((4, COLS)), dma((4, COLS)),
            dma((COLS,)), dma((COLS,)),
        ],
        compiler_params=pltpu.CompilerParams(
            collective_id=0, has_side_effects=True, vmem_limit_bytes=60 * 1024 * 1024
        ),
        name="spanned",
    )(
        page_owner.reshape(1, PAGES), page_slot, jnp.asarray(frequency), query_raw[0],
        suffix_keyval[0], query_gain[None], key_norm_gain[None], prefix_length, cache_pool[0],
    )
    return result.astype(BF16)[None]


def solution(mesh):
    finer = Mesh(mesh.devices.reshape(GROUPS, ROWS, COLS), ("group", "ctx_0", "ctx_1"))
    ctx = ("ctx_0", "ctx_1")
    in_specs = (
        P("group", ctx, None),
        P("group", ctx, None),
        P(),
        P(),
        P("group", ctx),
        P("group"),
        P("group", ctx, None),
        P("group", ctx),
        P("group", ctx, None, None),
    )
    return jax.shard_map(
        shards, mesh=finer, in_specs=in_specs, out_specs=P("group", ctx, None), check_vma=False
    )
```

```python
import jax
import jax.numpy as jnp
import numpy as np
from jax import lax
from jax.experimental import pallas as pl
from jax.experimental.pallas import tpu as pltpu
from jax.sharding import Mesh
from jax.sharding import PartitionSpec as P

MESH = pl.DeviceIdType.MESH
EPS = 1e-06
FLOOR = -65536.0
GROUPS = 8
ROWS = 8
COLS = 4
CAP = 12
PAGES = 48
POOL = 96
PAGE = 16
HEAD = 128
TOKENS = 16
RATIO = 8
KEYS = PAGES * PAGE
BLOCK = COLS * RATIO * TOKENS
HALF = BLOCK // 2
SUMROWS = 8
WIDE = KEYS + HEAD
PAIR = 2 * KEYS
CUT = 384
LAST = (4, 3, 5, 2, 6, 1, 7, 0)
QUARTERS = (2, 1, 3, 0)
FIRST_UP = (0, 1)
FIRST_DOWN = (2, 3)
F32 = jnp.float32
BF16 = jnp.bfloat16


def rot(a, n):
    return lax.rem(a, jnp.int32(n))


def kernel(
    owner, slots, freq, qraw_any, skv_any, qgain, kgain, plen, pool_any, out,
    qraw, skv, mix, tab, pool, send0, send1, send2, send3, recv0, recv1, recv2, recv3,
    near0, near1, near2, near3, cut1, cut2, cut3,
    kc, vt, sa, sb, pa, pb, qsend, qbuf, oacc, mref, osend, upin, dnin, upend, dnend, ownend,
    reqs,
    psend, precv, lsem, rsend, rrecv, ssem, xsend, xrecv,
    upsend, uprecv, dnsend, dnrecv, nsend, nrecv, uosend, uorecv, dosend, dorecv, fsem, frsem,
):
    g = lax.axis_index("group")
    z = lax.axis_index("ctx_0")
    x = lax.axis_index("ctx_1")
    sends = (send0, send1, send2, send3)
    recvs = (recv0, recv1, recv2, recv3)
    nears = (near0, near1, near2, near3)
    cuts = (near0, cut1, cut2, cut3)
    limit = plen[0]
    turn = 1 + 2 * rot(g, 2)
    up_z, down_z = rot(z + 1, ROWS), rot(z + ROWS - 1, ROWS)

    load_q = pltpu.make_async_copy(qraw_any, qraw, lsem.at[COLS + 1])
    load_kv = pltpu.make_async_copy(skv_any, skv, lsem.at[COLS + 2])
    load_pool = pltpu.make_async_copy(pool_any, pool, lsem.at[COLS])
    load_q.start()
    load_kv.start()
    load_pool.start()
    barrier = pltpu.get_barrier_semaphore()
    partners = [(rot(g + n, GROUPS), z, x) for n in range(1, GROUPS)]
    partners += [(g, z, rot(x + n, COLS)) for n in range(1, COLS)]
    partners += [(g, to_z, rot(x + n, COLS)) for n in range(COLS) for to_z in (up_z, down_z)]
    for to in partners:
        pl.semaphore_signal(barrier, inc=1, device_id=to, device_id_type=MESH)

    mix[...] = jnp.full((8, HEAD), -1, jnp.int32)
    mix[0:1, 0:PAGES] = owner[...]
    mix[1:2, 0:PAGES] = slots[...]
    lane = lax.broadcasted_iota(jnp.int32, (HEAD, HEAD), 1)
    line = lax.broadcasted_iota(jnp.int32, (HEAD, HEAD), 0)
    owners = jnp.broadcast_to(mix[0:1, :], (HEAD, HEAD))
    earlier = (owners == owners.T) & (line < lane)
    rank = jnp.sum(jnp.where(earlier, 1, 0), axis=0, keepdims=True)
    place = mix[0:1, :] * CAP + rank
    places = jnp.broadcast_to(place, (HEAD, HEAD)).T
    named = jnp.broadcast_to(mix[1:2, :], (HEAD, HEAD)).T
    wanted = (places == lane) & (line < PAGES)
    tab[0:1, :] = jnp.sum(jnp.where(wanted, named, 0), axis=0, keepdims=True)
    tab[1:2, :] = place
    tab[2:8, :] = jnp.zeros((6, HEAD), jnp.int32)

    token_at = limit + (z * COLS + x) * TOKENS + lax.broadcasted_iota(jnp.int32, (TOKENS, HEAD), 0)
    angles = token_at.astype(F32) * freq[...]
    cosf = jnp.cos(angles)
    sinf = jnp.sin(angles)
    upper = lax.broadcasted_iota(jnp.int32, (TOKENS, HEAD), 1) >= HEAD // 2
    sinf = jnp.where(upper, sinf, -sinf)
    scale = HEAD ** (-0.5) * 1.4426950408889634

    def turned(raw, gain):
        raw = raw.astype(F32)
        mean = jnp.mean(raw * raw, axis=-1, keepdims=True)
        flat = raw * lax.rsqrt(mean + EPS) * gain
        return flat * cosf + pltpu.roll(flat, HEAD // 2, 1) * sinf

    load_q.wait()
    load_kv.wait()
    for i in range(COLS * RATIO):
        part = turned(qraw[:, i * HEAD : (i + 1) * HEAD], qgain[...])
        qsend[i // RATIO, i % RATIO] = (part * scale).astype(BF16)
    for i in range(COLS):
        part = turned(skv[:, i * HEAD : (i + 1) * HEAD], kgain[...])
        qsend[i, RATIO] = part.astype(BF16)
        qsend[i, RATIO + 1] = skv[:, (COLS + i) * HEAD : (COLS + i + 1) * HEAD]

    pl.semaphore_wait(barrier, len(partners))

    def req_copy(d):
        to = rot(g + d, GROUPS)
        return pltpu.make_async_remote_copy(
            src_ref=tab, dst_ref=reqs.at[g], send_sem=rsend.at[d], recv_sem=rrecv.at[d],
            device_id=(to, z, x), device_id_type=MESH,
        )

    mine = z * COLS + x

    def q_copy(k):
        to = rot(x + k, COLS)
        return pltpu.make_async_remote_copy(
            src_ref=qsend.at[to], dst_ref=qbuf.at[mine], send_sem=xsend.at[k], recv_sem=xrecv.at[k],
            device_id=(g, z, to), device_id_type=MESH,
        )

    for d in range(1, GROUPS):
        req_copy(d).start()
    for k in range(1, COLS):
        q_copy(k).start()

    def ring_copy(s, k, up):
        col = rot(x + COLS - k, COLS)
        away = rot(z + ROWS - s, ROWS) if up else rot(z + s, ROWS)
        place = away * COLS + col
        if s == 0 and k == 0:
            src = qsend.at[x, pl.ds(0, RATIO + 1)]
        else:
            src = qbuf.at[place, pl.ds(0, RATIO + 1)]
        return pltpu.make_async_remote_copy(
            src_ref=src, dst_ref=qbuf.at[place, pl.ds(0, RATIO + 1)],
            send_sem=(upsend if up else dnsend).at[s, k],
            recv_sem=(uprecv if up else dnrecv).at[s, k],
            device_id=(g, up_z if up else down_z, x), device_id_type=MESH,
        )

    ring_copy(0, 0, True).start()
    ring_copy(0, 0, False).start()
    qbuf[mine] = qsend[x]

    own_req = pltpu.make_async_copy(tab, reqs.at[g], ssem.at[0])
    own_req.start()

    for d in range(1, GROUPS):
        req_copy(d).wait_recv()
    own_req.wait()
    load_pool.wait()

    def page_copy(k, d):
        to = rot(g + d, GROUPS)
        return pltpu.make_async_remote_copy(
            src_ref=sends[k].at[pl.ds(to * CAP, CAP)], dst_ref=recvs[k].at[pl.ds(g * CAP, CAP)],
            send_sem=psend.at[k, d], recv_sem=precv.at[k, d],
            device_id=(to, z, x), device_id_type=MESH,
        )

    def own_pages(k):
        own = pl.ds(g * CAP, CAP)
        return pltpu.make_async_copy(sends[k].at[own], recvs[k].at[own], lsem.at[k])

    def gather(k):
        @pl.loop(0, GROUPS)
        def _(d):
            to = rot(g + d, GROUPS)
            head = rot(x + k * (1 + 2 * rot(to, 2)), COLS)
            key_at = pl.multiple_of(head * HEAD, HEAD)
            value_at = pl.multiple_of((COLS + head) * HEAD, HEAD)
            for r in range(CAP):
                slot = reqs[to, 0, g * CAP + r]
                sends[k][to * CAP + r, :, 0:HEAD] = pool[slot, :, pl.ds(key_at, HEAD)]
                sends[k][to * CAP + r, :, HEAD : 2 * HEAD] = pool[slot, :, pl.ds(value_at, HEAD)]

            @pl.when(d > 0)
            def _():
                page_copy(k, d).start()

        own_pages(k).start()

    for k in (1, 2, 3, 0):
        gather(k)

    def near_copy(k):
        return pltpu.make_async_remote_copy(
            src_ref=cuts[k], dst_ref=nears[k], send_sem=nsend.at[k], recv_sem=nrecv.at[k],
            device_id=(g, z, rot(x + k * turn, COLS)), device_id_type=MESH,
        )

    def compact(k):
        for d in range(1, GROUPS):
            page_copy(k, d).wait_recv()
        own_pages(k).wait()

        @pl.loop(0, PAGES // 4)
        def _(j):
            for i in range(4):
                rows = pl.ds(pl.multiple_of((j * 4 + i) * PAGE, PAGE), PAGE)
                cuts[k][rows, :] = recvs[k][reqs[g, 1, j * 4 + i]]

        if k:
            near_copy(k).start()

    for k in range(1, COLS):
        q_copy(k).wait_recv()
        ring_copy(0, k, True).start()
        ring_copy(0, k, False).start()
    for s in range(1, 5):
        for k in range(COLS):
            if s < 4 or k in FIRST_UP:
                ring_copy(s - 1, k, True).wait_recv()
            if s < 3 or (s == 3 and k in FIRST_UP):
                ring_copy(s, k, True).start()
            if s < 4 or k in FIRST_DOWN:
                ring_copy(s - 1, k, False).wait_recv()
            if s < 3 or (s == 3 and k in FIRST_DOWN):
                ring_copy(s, k, False).start()
        if s == 2:
            compact(1)

    def queries(zb, c):
        part = qbuf[pl.ds(zb * COLS + 2 * c, 2), 0:RATIO]
        return part.reshape(HALF, HEAD)

    for b in range(COLS):
        rows = slice(KEYS + b * TOKENS, KEYS + (b + 1) * TOKENS)
        kc[rows, :] = qbuf[z * COLS + b, RATIO]
    kc[KEYS + COLS * TOKENS : WIDE, :] = jnp.zeros((HEAD - COLS * TOKENS, HEAD), BF16)
    suffix_v = [qbuf[z * COLS + b, RATIO + 1].astype(F32) for b in range(COLS)]
    suffix_v = jnp.concatenate(suffix_v + [jnp.zeros((HEAD - COLS * TOKENS, HEAD), F32)], axis=0)
    vt[0:HEAD, KEYS:WIDE] = suffix_v.T.astype(BF16)
    vt[HEAD:, KEYS:WIDE] = jnp.ones((SUMROWS, HEAD), BF16)

    shared_key = qbuf[0, RATIO][0:1, :].astype(F32)

    def prepare(k, start=0):
        base = (z * COLS + rot(x + 3 * COLS - k * turn, COLS)) * KEYS
        for b in range(KEYS // HEAD):
            rows = slice(b * HEAD, (b + 1) * HEAD)
            token = base + b * HEAD + lax.broadcasted_iota(jnp.int32, (HEAD, HEAD), 0)
            seen = token < limit
            keys = nears[k][rows, 0:HEAD].astype(F32)
            values = nears[k][rows, HEAD:].astype(F32)
            put = slice(start + b * HEAD, start + (b + 1) * HEAD)
            kc[put, :] = jnp.where(seen, keys, shared_key).astype(BF16)
            vt[0:HEAD, put] = jnp.where(seen, values, 0.0).T.astype(BF16)
        lane = base + lax.broadcasted_iota(jnp.int32, (SUMROWS, KEYS), 1)
        vt[HEAD:, start : start + KEYS] = jnp.where(lane < limit, 1.0, 0.0).astype(BF16)

    def scores(dst, peak, zb, c, first):
        step(None, None, 0, 0, dst, peak, zb, c, first)

    def finish(src, peak, zb, c, first):
        step(src, peak, zb, c, None, None, 0, 0, first)

    def step(src, src_peak, zb, c, dst, dst_peak, next_zb, next_c, first):
        size = WIDE if first else KEYS
        size = PAIR if first is None else size
        if src is not None:
            top = src_peak[0:1, :]
            if not first:
                before = jnp.concatenate([mref[zb, q, 0:1, :] for q in (2 * c, 2 * c + 1)], axis=1)
                top = jnp.maximum(before, top)
        if dst is not None:
            asked = queries(next_zb, next_c)
        weights, tops = [], []
        for lo in range(0, size, CUT):
            hi = min(lo + CUT, size)
            if dst is not None:
                s = lax.dot_general(
                    kc[lo:hi, :], asked, (((1,), (1,)), ((), ())), preferred_element_type=F32
                )
                if first and hi > KEYS:
                    key_row = lax.broadcasted_iota(jnp.int32, (hi - lo, HALF), 0) + (lo - KEYS)
                    column = lax.broadcasted_iota(jnp.int32, (hi - lo, HALF), 1)
                    asker = next_zb * (COLS * TOKENS) + (column // HEAD + 2 * next_c) * TOKENS
                    asker = asker + (column & (TOKENS - 1))
                    seen = (key_row < COLS * TOKENS) & (z * (COLS * TOKENS) + key_row <= asker)
                    s = jnp.where((key_row < 0) | seen, s, FLOOR)
                dst[lo:hi, :] = s
                tops.append(jnp.max(s, axis=0, keepdims=True))
            if src is not None:
                weights.append(jnp.exp2(src[lo:hi, :] - top).astype(BF16))
        if dst is not None:
            best = tops[0]
            for t in tops[1:]:
                best = jnp.maximum(best, t)
            dst_peak[0:1, :] = jnp.ceil(best * 0.25) * 4.0
        if src is not None:
            fresh = jnp.dot(vt[:, 0:size], jnp.concatenate(weights, axis=0), preferred_element_type=F32)
            for i in range(2):
                q, at = 2 * c + i, slice(i * HEAD, (i + 1) * HEAD)
                part = fresh[:, at]
                if not first:
                    part = oacc[zb, q] * jnp.exp2(before[:, at] - top[:, at]) + part
                oacc[zb, q] = part
                mref[zb, q, 0:1, :] = top[:, at]

    def attend(k, first):
        if k:
            near_copy(k).wait_recv()
        prepare(k)
        scores(sa, pa, 0, 0, first)

        @pl.loop(0, ROWS)
        def _(zb):
            step(sa, pa, zb, 0, sb, pb, zb, 1, first)
            step(sb, pb, zb, 1, sa, pa, jnp.minimum(zb + 1, ROWS - 1), 0, first)

    def quarter(j):
        return rot(x + QUARTERS[j], COLS)

    def sum_copy(s, j, up):
        block = rot(z + 4 - s, ROWS) if up else rot(z + 4 + s, ROWS)
        if s < 3:
            dst, to_x = (upin if up else dnin).at[s, j], x
        else:
            dst, to_x = (upend if up else dnend).at[x], quarter(j)
        return pltpu.make_async_remote_copy(
            src_ref=osend.at[block, quarter(j)], dst_ref=dst,
            send_sem=(uosend if up else dosend).at[s, j],
            recv_sem=(uorecv if up else dorecv).at[s, j],
            device_id=(g, up_z if up else down_z, to_x), device_id_type=MESH,
        )

    def own_copy(j):
        return pltpu.make_async_remote_copy(
            src_ref=osend.at[z, quarter(j)], dst_ref=ownend.at[x],
            send_sem=fsem.at[j], recv_sem=frsem.at[j],
            device_id=(g, z, quarter(j)), device_id_type=MESH,
        )

    def own_part(zb, q):
        return oacc[zb, q, 0:HEAD, :], mref[zb, q, 0:1, :], oacc[zb, q, HEAD : HEAD + 1, :]

    def join(part, arrived):
        o, m, l = part
        tile = arrived[HEAD:, :].astype(F32)
        m_in = tile[0:1]
        l_in = tile[1:2] + tile[2:3]
        top = jnp.maximum(m, m_in)
        mul, mul_in = jnp.exp2(m - top), jnp.exp2(m_in - top)
        return o * mul + arrived[0:HEAD, :].astype(F32) * mul_in, top, l * mul + l_in * mul_in

    def pack(zb, q, part):
        o, m, l = part
        l_high = l.astype(BF16).astype(F32)
        row = lax.broadcasted_iota(jnp.int32, (SUMROWS, HEAD), 0)
        tile = jnp.where(row == 0, m, jnp.where(row == 1, l_high, jnp.where(row == 2, l - l_high, 0.0)))
        osend[zb, q, 0:HEAD, :] = o.astype(BF16)
        osend[zb, q, HEAD:, :] = tile.astype(BF16)

    def relay(s, early, late):
        for js in zip(early, late):
            for up, j in zip((True, False), js):
                block = rot(z + 4 - s, ROWS) if up else rot(z + 4 + s, ROWS)
                q = quarter(j)
                part = own_part(block, q)
                if s > 1 or (s == 1 and j in (FIRST_UP if up else FIRST_DOWN)):
                    sum_copy(s - 1, j, up).wait_recv()
                    part = join(part, (upin if up else dnin).at[s - 1, j])
                pack(block, q, part)
                sum_copy(s, j, up).start()

    compact(2)
    attend(1, True)
    compact(3)
    attend(2, False)

    near_copy(3).wait_recv()
    prepare(3)
    compact(0)
    prepare(0, KEYS)

    def block_at(n):
        return rot(z + LAST[n], ROWS)

    scores(sa, pa, block_at(0), 0, None)
    for n in range(ROWS):
        step(sa, pa, block_at(n), 0, sb, pb, block_at(n), 1, None)
        if n < ROWS - 1:
            step(sb, pb, block_at(n), 1, sa, pa, block_at(n + 1), 0, None)
        else:
            finish(sb, pb, block_at(n), 1, None)
        if n == 0:
            relay(0, FIRST_UP, FIRST_DOWN)
        if n == 2:
            relay(1, FIRST_DOWN, FIRST_UP)
        if n == 3:
            relay(1, FIRST_UP, FIRST_DOWN)
        if n == 5:
            relay(2, FIRST_DOWN, FIRST_UP)
        if n == 6:
            relay(2, FIRST_UP, FIRST_DOWN)
    for j in range(COLS):
        pack(z, quarter(j), own_part(z, quarter(j)))
        if QUARTERS[j]:
            own_copy(j).start()
    ownend[x] = osend[z, x]
    relay(3, FIRST_DOWN, FIRST_UP)
    relay(3, FIRST_UP, FIRST_DOWN)

    for j in range(COLS):
        if QUARTERS[j]:
            own_copy(j).wait_recv()
        sum_copy(3, j, False).wait_recv()
        sum_copy(3, j, True).wait_recv()
    for h in range(COLS):
        tile = ownend[h, HEAD:, :].astype(F32)
        part = (ownend[h, 0:HEAD, :].astype(F32), tile[0:1], tile[1:2] + tile[2:3])
        o, m, l = join(join(part, dnend.at[h]), upend.at[h])
        rows = (o / l).T.astype(BF16).astype(F32)
        for i in range(RATIO):
            at = (h * RATIO + i) * HEAD
            out[:, at : at + HEAD] = rows[i * TOKENS : (i + 1) * TOKENS]

    for d in range(1, GROUPS):
        req_copy(d).wait_send()
    for k in range(1, COLS):
        q_copy(k).wait_send()
        near_copy(k).wait_send()
        own_copy(k - 1).wait_send()
    for s in range(4):
        for k in range(COLS):
            if s < 3 or k in FIRST_UP:
                ring_copy(s, k, True).wait_send()
            if s < 3 or k in FIRST_DOWN:
                ring_copy(s, k, False).wait_send()
            if s or k in FIRST_UP:
                sum_copy(s, k, True).wait_send()
            if s or k in FIRST_DOWN:
                sum_copy(s, k, False).wait_send()
    for k in range(COLS):
        for d in range(1, GROUPS):
            page_copy(k, d).wait_send()


def shards(
    query_raw, suffix_keyval, query_gain, key_norm_gain, positions, prefix_length,
    page_owner, page_slot, cache_pool,
):
    half = np.arange(HEAD) % (HEAD // 2)
    frequency = (1000000.0 ** (-(2.0 / HEAD) * half)).astype(np.float32)[None]
    vmem = pl.BlockSpec(memory_space=pltpu.VMEM)
    far = pl.BlockSpec(memory_space=pl.ANY)
    page_half = (GROUPS * CAP, PAGE, 2 * HEAD)
    dma = pltpu.SemaphoreType.DMA
    result = pl.pallas_call(
        kernel,
        out_shape=jax.ShapeDtypeStruct((TOKENS, COLS * RATIO * HEAD), F32),
        in_specs=[vmem] * 3 + [far] * 2 + [vmem] * 2 + [pl.BlockSpec(memory_space=pltpu.SMEM), far],
        out_specs=vmem,
        scratch_shapes=[
            pltpu.VMEM((TOKENS, COLS * RATIO * HEAD), BF16),
            pltpu.VMEM((TOKENS, 2 * COLS * HEAD), BF16),
            pltpu.VMEM((8, HEAD), jnp.int32),
            pltpu.VMEM((8, HEAD), jnp.int32),
        ]
        + [pltpu.VMEM((POOL, PAGE, 2 * COLS * HEAD), BF16)]
        + [pltpu.VMEM(page_half, BF16)] * 8
        + [pltpu.VMEM((KEYS, 2 * HEAD), BF16)] * 7
        + [
            pltpu.VMEM((PAIR, HEAD), BF16),
            pltpu.VMEM((HEAD + SUMROWS, PAIR), BF16),
            pltpu.VMEM((PAIR, HALF), F32),
            pltpu.VMEM((PAIR, HALF), F32),
            pltpu.VMEM((8, HALF), F32),
            pltpu.VMEM((8, HALF), F32),
            pltpu.VMEM((COLS, RATIO + 2, TOKENS, HEAD), BF16),
            pltpu.VMEM((ROWS * COLS, RATIO + 2, TOKENS, HEAD), BF16),
            pltpu.VMEM((ROWS, COLS, HEAD + SUMROWS, HEAD), F32),
            pltpu.VMEM((ROWS, COLS, 8, HEAD), F32),
            pltpu.VMEM((ROWS, COLS, HEAD + SUMROWS, HEAD), BF16),
            pltpu.VMEM((3, COLS, HEAD + SUMROWS, HEAD), BF16),
            pltpu.VMEM((3, COLS, HEAD + SUMROWS, HEAD), BF16),
            pltpu.VMEM((COLS, HEAD + SUMROWS, HEAD), BF16),
            pltpu.VMEM((COLS, HEAD + SUMROWS, HEAD), BF16),
            pltpu.VMEM((COLS, HEAD + SUMROWS, HEAD), BF16),
            pltpu.SMEM((GROUPS, 8, HEAD), jnp.int32),
            dma((COLS, GROUPS)), dma((COLS, GROUPS)), dma((COLS + 3,)),
            dma((GROUPS,)), dma((GROUPS,)), dma((GROUPS,)),
            dma((COLS,)), dma((COLS,)),
            dma((4, COLS)), dma((4, COLS)), dma((4, COLS)), dma((4, COLS)),
            dma((COLS,)), dma((COLS,)),
            dma((4, COLS)), dma((4, COLS)), dma((4, COLS)), dma((4, COLS)),
            dma((COLS,)), dma((COLS,)),
        ],
        compiler_params=pltpu.CompilerParams(
            collective_id=0, has_side_effects=True, vmem_limit_bytes=60 * 1024 * 1024
        ),
        name="spanned",
    )(
        page_owner.reshape(1, PAGES), page_slot, jnp.asarray(frequency), query_raw[0],
        suffix_keyval[0], query_gain[None], key_norm_gain[None], prefix_length, cache_pool[0],
    )
    return result.astype(BF16)[None]


def solution(mesh):
    finer = Mesh(mesh.devices.reshape(GROUPS, ROWS, COLS), ("group", "ctx_0", "ctx_1"))
    ctx = ("ctx_0", "ctx_1")
    in_specs = (
        P("group", ctx, None),
        P("group", ctx, None),
        P(),
        P(),
        P("group", ctx),
        P("group"),
        P("group", ctx, None),
        P("group", ctx),
        P("group", ctx, None, None),
    )
    return jax.shard_map(
        shards, mesh=finer, in_specs=in_specs, out_specs=P("group", ctx, None), check_vma=False
    )
```

```python
import jax
import jax.numpy as jnp
import numpy as np
from jax import lax
from jax.experimental import pallas as pl
from jax.experimental.pallas import tpu as pltpu
from jax.sharding import Mesh
from jax.sharding import PartitionSpec as P

MESH = pl.DeviceIdType.MESH
EPS = 1e-06
FLOOR = -65536.0
GROUPS = 8
ROWS = 8
COLS = 4
CAP = 12
PAGES = 48
POOL = 96
PAGE = 16
HEAD = 128
TOKENS = 16
RATIO = 8
KEYS = PAGES * PAGE
BLOCK = COLS * RATIO * TOKENS
HALF = BLOCK // 2
SUMROWS = 8
WIDE = KEYS + HEAD
PAIR = 2 * KEYS
CUT = 384
LAST = (4, 3, 5, 2, 6, 1, 7, 0)
QUARTERS = (2, 1, 3, 0)
FIRST_UP = (0, 1)
FIRST_DOWN = (2, 3)
F32 = jnp.float32
BF16 = jnp.bfloat16


def rot(a, n):
    return lax.rem(a, jnp.int32(n))


def kernel(
    owner, slots, freq, qraw_any, skv_any, qgain, kgain, plen, pool_any, out,
    qraw, skv, mix, tab, pool, send0, send1, send2, send3, recv0, recv1, recv2, recv3,
    near0, near1, near2, near3, cut1, cut2, cut3,
    kc, vt, sa, sb, pa, pb, qsend, qbuf, oacc, mref, osend, upin, dnin, upend, dnend, ownend,
    reqs,
    psend, precv, lsem, rsend, rrecv, ssem, xsend, xrecv,
    upsend, uprecv, dnsend, dnrecv, nsend, nrecv, uosend, uorecv, dosend, dorecv, fsem, frsem,
):
    g = lax.axis_index("group")
    z = lax.axis_index("ctx_0")
    x = lax.axis_index("ctx_1")
    sends = (send0, send1, send2, send3)
    recvs = (recv0, recv1, recv2, recv3)
    nears = (near0, near1, near2, near3)
    cuts = (near0, cut1, cut2, cut3)
    limit = plen[0]
    turn = 1 + 2 * rot(g, 2)
    up_z, down_z = rot(z + 1, ROWS), rot(z + ROWS - 1, ROWS)

    load_q = pltpu.make_async_copy(qraw_any, qraw, lsem.at[COLS + 1])
    load_kv = pltpu.make_async_copy(skv_any, skv, lsem.at[COLS + 2])
    load_pool = pltpu.make_async_copy(pool_any, pool, lsem.at[COLS])
    load_q.start()
    load_kv.start()
    load_pool.start()
    barrier = pltpu.get_barrier_semaphore()
    partners = [(rot(g + n, GROUPS), z, x) for n in range(1, GROUPS)]
    partners += [(g, z, rot(x + n, COLS)) for n in range(1, COLS)]
    partners += [(g, to_z, rot(x + n, COLS)) for n in range(COLS) for to_z in (up_z, down_z)]
    for to in partners:
        pl.semaphore_signal(barrier, inc=1, device_id=to, device_id_type=MESH)

    mix[...] = jnp.full((8, HEAD), -1, jnp.int32)
    mix[0:1, 0:PAGES] = owner[...]
    mix[1:2, 0:PAGES] = slots[...]
    lane = lax.broadcasted_iota(jnp.int32, (HEAD, HEAD), 1)
    line = lax.broadcasted_iota(jnp.int32, (HEAD, HEAD), 0)
    owners = jnp.broadcast_to(mix[0:1, :], (HEAD, HEAD))
    earlier = (owners == owners.T) & (line < lane)
    rank = jnp.sum(jnp.where(earlier, 1, 0), axis=0, keepdims=True)
    place = mix[0:1, :] * CAP + rank
    places = jnp.broadcast_to(place, (HEAD, HEAD)).T
    named = jnp.broadcast_to(mix[1:2, :], (HEAD, HEAD)).T
    wanted = (places == lane) & (line < PAGES)
    tab[0:1, :] = jnp.sum(jnp.where(wanted, named, 0), axis=0, keepdims=True)
    tab[1:2, :] = place
    tab[2:8, :] = jnp.zeros((6, HEAD), jnp.int32)

    pl.semaphore_wait(barrier, len(partners))

    def req_copy(d):
        to = rot(g + d, GROUPS)
        return pltpu.make_async_remote_copy(
            src_ref=tab, dst_ref=reqs.at[g], send_sem=rsend.at[d], recv_sem=rrecv.at[d],
            device_id=(to, z, x), device_id_type=MESH,
        )

    for d in range(1, GROUPS):
        req_copy(d).start()

    token_at = limit + (z * COLS + x) * TOKENS + lax.broadcasted_iota(jnp.int32, (TOKENS, HEAD), 0)
    angles = token_at.astype(F32) * freq[...]
    cosf = jnp.cos(angles)
    sinf = jnp.sin(angles)
    upper = lax.broadcasted_iota(jnp.int32, (TOKENS, HEAD), 1) >= HEAD // 2
    sinf = jnp.where(upper, sinf, -sinf)
    scale = HEAD ** (-0.5) * 1.4426950408889634

    def turned(raw, gain):
        raw = raw.astype(F32)
        mean = jnp.mean(raw * raw, axis=-1, keepdims=True)
        flat = raw * lax.rsqrt(mean + EPS) * gain
        return flat * cosf + pltpu.roll(flat, HEAD // 2, 1) * sinf

    load_q.wait()
    load_kv.wait()
    for i in range(COLS * RATIO):
        part = turned(qraw[:, i * HEAD : (i + 1) * HEAD], qgain[...])
        qsend[i // RATIO, i % RATIO] = (part * scale).astype(BF16)
    for i in range(COLS):
        part = turned(skv[:, i * HEAD : (i + 1) * HEAD], kgain[...])
        qsend[i, RATIO] = part.astype(BF16)
        qsend[i, RATIO + 1] = skv[:, (COLS + i) * HEAD : (COLS + i + 1) * HEAD]

    mine = z * COLS + x

    def q_copy(k):
        to = rot(x + k, COLS)
        return pltpu.make_async_remote_copy(
            src_ref=qsend.at[to], dst_ref=qbuf.at[mine], send_sem=xsend.at[k], recv_sem=xrecv.at[k],
            device_id=(g, z, to), device_id_type=MESH,
        )

    for k in range(1, COLS):
        q_copy(k).start()

    def ring_copy(s, k, up):
        col = rot(x + COLS - k, COLS)
        away = rot(z + ROWS - s, ROWS) if up else rot(z + s, ROWS)
        place = away * COLS + col
        if s == 0 and k == 0:
            src = qsend.at[x, pl.ds(0, RATIO + 1)]
        else:
            src = qbuf.at[place, pl.ds(0, RATIO + 1)]
        return pltpu.make_async_remote_copy(
            src_ref=src, dst_ref=qbuf.at[place, pl.ds(0, RATIO + 1)],
            send_sem=(upsend if up else dnsend).at[s, k],
            recv_sem=(uprecv if up else dnrecv).at[s, k],
            device_id=(g, up_z if up else down_z, x), device_id_type=MESH,
        )

    ring_copy(0, 0, True).start()
    ring_copy(0, 0, False).start()
    qbuf[mine] = qsend[x]

    own_req = pltpu.make_async_copy(tab, reqs.at[g], ssem.at[0])
    own_req.start()

    for d in range(1, GROUPS):
        req_copy(d).wait_recv()
    own_req.wait()
    load_pool.wait()

    def page_copy(k, d):
        to = rot(g + d, GROUPS)
        return pltpu.make_async_remote_copy(
            src_ref=sends[k].at[pl.ds(to * CAP, CAP)], dst_ref=recvs[k].at[pl.ds(g * CAP, CAP)],
            send_sem=psend.at[k, d], recv_sem=precv.at[k, d],
            device_id=(to, z, x), device_id_type=MESH,
        )

    def own_pages(k):
        own = pl.ds(g * CAP, CAP)
        return pltpu.make_async_copy(sends[k].at[own], recvs[k].at[own], lsem.at[k])

    def gather(k):
        @pl.loop(0, GROUPS)
        def _(d):
            to = rot(g + d, GROUPS)
            head = rot(x + k * (1 + 2 * rot(to, 2)), COLS)
            key_at = pl.multiple_of(head * HEAD, HEAD)
            value_at = pl.multiple_of((COLS + head) * HEAD, HEAD)
            for r in range(CAP):
                slot = reqs[to, 0, g * CAP + r]
                sends[k][to * CAP + r, :, 0:HEAD] = pool[slot, :, pl.ds(key_at, HEAD)]
                sends[k][to * CAP + r, :, HEAD : 2 * HEAD] = pool[slot, :, pl.ds(value_at, HEAD)]

            @pl.when(d > 0)
            def _():
                page_copy(k, d).start()

        own_pages(k).start()

    for k in (1, 2, 3, 0):
        gather(k)

    def near_copy(k):
        return pltpu.make_async_remote_copy(
            src_ref=cuts[k], dst_ref=nears[k], send_sem=nsend.at[k], recv_sem=nrecv.at[k],
            device_id=(g, z, rot(x + k * turn, COLS)), device_id_type=MESH,
        )

    def compact(k):
        for d in range(1, GROUPS):
            page_copy(k, d).wait_recv()
        own_pages(k).wait()

        @pl.loop(0, PAGES // 4)
        def _(j):
            for i in range(4):
                rows = pl.ds(pl.multiple_of((j * 4 + i) * PAGE, PAGE), PAGE)
                cuts[k][rows, :] = recvs[k][reqs[g, 1, j * 4 + i]]

        if k:
            near_copy(k).start()

    for k in range(1, COLS):
        q_copy(k).wait_recv()
        ring_copy(0, k, True).start()
        ring_copy(0, k, False).start()
    for s in range(1, 5):
        for k in range(COLS):
            if s < 4 or k in FIRST_UP:
                ring_copy(s - 1, k, True).wait_recv()
            if s < 3 or (s == 3 and k in FIRST_UP):
                ring_copy(s, k, True).start()
            if s < 4 or k in FIRST_DOWN:
                ring_copy(s - 1, k, False).wait_recv()
            if s < 3 or (s == 3 and k in FIRST_DOWN):
                ring_copy(s, k, False).start()
        if s == 2:
            compact(1)

    def queries(zb, c):
        part = qbuf[pl.ds(zb * COLS + 2 * c, 2), 0:RATIO]
        return part.reshape(HALF, HEAD)

    for b in range(COLS):
        rows = slice(KEYS + b * TOKENS, KEYS + (b + 1) * TOKENS)
        kc[rows, :] = qbuf[z * COLS + b, RATIO]
    kc[KEYS + COLS * TOKENS : WIDE, :] = jnp.zeros((HEAD - COLS * TOKENS, HEAD), BF16)
    suffix_v = [qbuf[z * COLS + b, RATIO + 1].astype(F32) for b in range(COLS)]
    suffix_v = jnp.concatenate(suffix_v + [jnp.zeros((HEAD - COLS * TOKENS, HEAD), F32)], axis=0)
    vt[0:HEAD, KEYS:WIDE] = suffix_v.T.astype(BF16)
    vt[HEAD:, KEYS:WIDE] = jnp.ones((SUMROWS, HEAD), BF16)

    shared_key = qbuf[0, RATIO][0:1, :].astype(F32)

    def prepare(k, start=0):
        base = (z * COLS + rot(x + 3 * COLS - k * turn, COLS)) * KEYS
        for b in range(KEYS // HEAD):
            rows = slice(b * HEAD, (b + 1) * HEAD)
            token = base + b * HEAD + lax.broadcasted_iota(jnp.int32, (HEAD, HEAD), 0)
            seen = token < limit
            keys = nears[k][rows, 0:HEAD].astype(F32)
            values = nears[k][rows, HEAD:].astype(F32)
            put = slice(start + b * HEAD, start + (b + 1) * HEAD)
            kc[put, :] = jnp.where(seen, keys, shared_key).astype(BF16)
            vt[0:HEAD, put] = jnp.where(seen, values, 0.0).T.astype(BF16)
        lane = base + lax.broadcasted_iota(jnp.int32, (SUMROWS, KEYS), 1)
        vt[HEAD:, start : start + KEYS] = jnp.where(lane < limit, 1.0, 0.0).astype(BF16)

    def scores(dst, peak, zb, c, first):
        step(None, None, 0, 0, dst, peak, zb, c, first)

    def finish(src, peak, zb, c, first):
        step(src, peak, zb, c, None, None, 0, 0, first)

    def step(src, src_peak, zb, c, dst, dst_peak, next_zb, next_c, first):
        size = WIDE if first else KEYS
        size = PAIR if first is None else size
        if src is not None:
            top = src_peak[0:1, :]
            if not first:
                before = jnp.concatenate([mref[zb, q, 0:1, :] for q in (2 * c, 2 * c + 1)], axis=1)
                top = jnp.maximum(before, top)
        if dst is not None:
            asked = queries(next_zb, next_c)
        weights, tops = [], []
        for lo in range(0, size, CUT):
            hi = min(lo + CUT, size)
            if dst is not None:
                s = lax.dot_general(
                    kc[lo:hi, :], asked, (((1,), (1,)), ((), ())), preferred_element_type=F32
                )
                if first and hi > KEYS:
                    key_row = lax.broadcasted_iota(jnp.int32, (hi - lo, HALF), 0) + (lo - KEYS)
                    column = lax.broadcasted_iota(jnp.int32, (hi - lo, HALF), 1)
                    asker = next_zb * (COLS * TOKENS) + (column // HEAD + 2 * next_c) * TOKENS
                    asker = asker + (column & (TOKENS - 1))
                    seen = (key_row < COLS * TOKENS) & (z * (COLS * TOKENS) + key_row <= asker)
                    s = jnp.where((key_row < 0) | seen, s, FLOOR)
                dst[lo:hi, :] = s
                tops.append(jnp.max(s, axis=0, keepdims=True))
            if src is not None:
                weights.append(jnp.exp2(src[lo:hi, :] - top).astype(BF16))
        if dst is not None:
            best = tops[0]
            for t in tops[1:]:
                best = jnp.maximum(best, t)
            dst_peak[0:1, :] = jnp.ceil(best * 0.25) * 4.0
        if src is not None:
            fresh = jnp.dot(vt[:, 0:size], jnp.concatenate(weights, axis=0), preferred_element_type=F32)
            for i in range(2):
                q, at = 2 * c + i, slice(i * HEAD, (i + 1) * HEAD)
                part = fresh[:, at]
                if not first:
                    part = oacc[zb, q] * jnp.exp2(before[:, at] - top[:, at]) + part
                oacc[zb, q] = part
                mref[zb, q, 0:1, :] = top[:, at]

    def attend(k, first):
        if k:
            near_copy(k).wait_recv()
        prepare(k)
        scores(sa, pa, 0, 0, first)

        @pl.loop(0, ROWS)
        def _(zb):
            step(sa, pa, zb, 0, sb, pb, zb, 1, first)
            step(sb, pb, zb, 1, sa, pa, jnp.minimum(zb + 1, ROWS - 1), 0, first)

    def quarter(j):
        return rot(x + QUARTERS[j], COLS)

    def sum_copy(s, j, up):
        block = rot(z + 4 - s, ROWS) if up else rot(z + 4 + s, ROWS)
        if s < 3:
            dst, to_x = (upin if up else dnin).at[s, j], x
        else:
            dst, to_x = (upend if up else dnend).at[x], quarter(j)
        return pltpu.make_async_remote_copy(
            src_ref=osend.at[block, quarter(j)], dst_ref=dst,
            send_sem=(uosend if up else dosend).at[s, j],
            recv_sem=(uorecv if up else dorecv).at[s, j],
            device_id=(g, up_z if up else down_z, to_x), device_id_type=MESH,
        )

    def own_copy(j):
        return pltpu.make_async_remote_copy(
            src_ref=osend.at[z, quarter(j)], dst_ref=ownend.at[x],
            send_sem=fsem.at[j], recv_sem=frsem.at[j],
            device_id=(g, z, quarter(j)), device_id_type=MESH,
        )

    def own_part(zb, q):
        return oacc[zb, q, 0:HEAD, :], mref[zb, q, 0:1, :], oacc[zb, q, HEAD : HEAD + 1, :]

    def join(part, arrived):
        o, m, l = part
        tile = arrived[HEAD:, :].astype(F32)
        m_in = tile[0:1]
        l_in = tile[1:2] + tile[2:3]
        top = jnp.maximum(m, m_in)
        mul, mul_in = jnp.exp2(m - top), jnp.exp2(m_in - top)
        return o * mul + arrived[0:HEAD, :].astype(F32) * mul_in, top, l * mul + l_in * mul_in

    def pack(zb, q, part):
        o, m, l = part
        l_high = l.astype(BF16).astype(F32)
        row = lax.broadcasted_iota(jnp.int32, (SUMROWS, HEAD), 0)
        tile = jnp.where(row == 0, m, jnp.where(row == 1, l_high, jnp.where(row == 2, l - l_high, 0.0)))
        osend[zb, q, 0:HEAD, :] = o.astype(BF16)
        osend[zb, q, HEAD:, :] = tile.astype(BF16)

    def relay(s, early, late):
        for js in zip(early, late):
            for up, j in zip((True, False), js):
                block = rot(z + 4 - s, ROWS) if up else rot(z + 4 + s, ROWS)
                q = quarter(j)
                part = own_part(block, q)
                if s > 1 or (s == 1 and j in (FIRST_UP if up else FIRST_DOWN)):
                    sum_copy(s - 1, j, up).wait_recv()
                    part = join(part, (upin if up else dnin).at[s - 1, j])
                pack(block, q, part)
                sum_copy(s, j, up).start()

    compact(2)
    attend(1, True)
    compact(3)
    attend(2, False)

    near_copy(3).wait_recv()
    prepare(3)
    compact(0)
    prepare(0, KEYS)

    def block_at(n):
        return rot(z + LAST[n], ROWS)

    scores(sa, pa, block_at(0), 0, None)
    for n in range(ROWS):
        step(sa, pa, block_at(n), 0, sb, pb, block_at(n), 1, None)
        if n < ROWS - 1:
            step(sb, pb, block_at(n), 1, sa, pa, block_at(n + 1), 0, None)
        else:
            finish(sb, pb, block_at(n), 1, None)
        if n == 0:
            relay(0, FIRST_UP, FIRST_DOWN)
        if n == 2:
            relay(1, FIRST_DOWN, FIRST_UP)
        if n == 3:
            relay(1, FIRST_UP, FIRST_DOWN)
        if n == 5:
            relay(2, FIRST_DOWN, FIRST_UP)
        if n == 6:
            relay(2, FIRST_UP, FIRST_DOWN)
    for j in range(COLS):
        pack(z, quarter(j), own_part(z, quarter(j)))
        if QUARTERS[j]:
            own_copy(j).start()
    ownend[x] = osend[z, x]
    relay(3, FIRST_DOWN, FIRST_UP)
    relay(3, FIRST_UP, FIRST_DOWN)

    for j in range(COLS):
        if QUARTERS[j]:
            own_copy(j).wait_recv()
        sum_copy(3, j, False).wait_recv()
        sum_copy(3, j, True).wait_recv()
    for h in range(COLS):
        tile = ownend[h, HEAD:, :].astype(F32)
        part = (ownend[h, 0:HEAD, :].astype(F32), tile[0:1], tile[1:2] + tile[2:3])
        o, m, l = join(join(part, dnend.at[h]), upend.at[h])
        rows = (o / l).T.astype(BF16).astype(F32)
        for i in range(RATIO):
            at = (h * RATIO + i) * HEAD
            out[:, at : at + HEAD] = rows[i * TOKENS : (i + 1) * TOKENS]

    for d in range(1, GROUPS):
        req_copy(d).wait_send()
    for k in range(1, COLS):
        q_copy(k).wait_send()
        near_copy(k).wait_send()
        own_copy(k - 1).wait_send()
    for s in range(4):
        for k in range(COLS):
            if s < 3 or k in FIRST_UP:
                ring_copy(s, k, True).wait_send()
            if s < 3 or k in FIRST_DOWN:
                ring_copy(s, k, False).wait_send()
            if s or k in FIRST_UP:
                sum_copy(s, k, True).wait_send()
            if s or k in FIRST_DOWN:
                sum_copy(s, k, False).wait_send()
    for k in range(COLS):
        for d in range(1, GROUPS):
            page_copy(k, d).wait_send()


def shards(
    query_raw, suffix_keyval, query_gain, key_norm_gain, positions, prefix_length,
    page_owner, page_slot, cache_pool,
):
    half = np.arange(HEAD) % (HEAD // 2)
    frequency = (1000000.0 ** (-(2.0 / HEAD) * half)).astype(np.float32)[None]
    vmem = pl.BlockSpec(memory_space=pltpu.VMEM)
    far = pl.BlockSpec(memory_space=pl.ANY)
    page_half = (GROUPS * CAP, PAGE, 2 * HEAD)
    dma = pltpu.SemaphoreType.DMA
    result = pl.pallas_call(
        kernel,
        out_shape=jax.ShapeDtypeStruct((TOKENS, COLS * RATIO * HEAD), F32),
        in_specs=[vmem] * 3 + [far] * 2 + [vmem] * 2 + [pl.BlockSpec(memory_space=pltpu.SMEM), far],
        out_specs=vmem,
        scratch_shapes=[
            pltpu.VMEM((TOKENS, COLS * RATIO * HEAD), BF16),
            pltpu.VMEM((TOKENS, 2 * COLS * HEAD), BF16),
            pltpu.VMEM((8, HEAD), jnp.int32),
            pltpu.VMEM((8, HEAD), jnp.int32),
        ]
        + [pltpu.VMEM((POOL, PAGE, 2 * COLS * HEAD), BF16)]
        + [pltpu.VMEM(page_half, BF16)] * 8
        + [pltpu.VMEM((KEYS, 2 * HEAD), BF16)] * 7
        + [
            pltpu.VMEM((PAIR, HEAD), BF16),
            pltpu.VMEM((HEAD + SUMROWS, PAIR), BF16),
            pltpu.VMEM((PAIR, HALF), F32),
            pltpu.VMEM((PAIR, HALF), F32),
            pltpu.VMEM((8, HALF), F32),
            pltpu.VMEM((8, HALF), F32),
            pltpu.VMEM((COLS, RATIO + 2, TOKENS, HEAD), BF16),
            pltpu.VMEM((ROWS * COLS, RATIO + 2, TOKENS, HEAD), BF16),
            pltpu.VMEM((ROWS, COLS, HEAD + SUMROWS, HEAD), F32),
            pltpu.VMEM((ROWS, COLS, 8, HEAD), F32),
            pltpu.VMEM((ROWS, COLS, HEAD + SUMROWS, HEAD), BF16),
            pltpu.VMEM((3, COLS, HEAD + SUMROWS, HEAD), BF16),
            pltpu.VMEM((3, COLS, HEAD + SUMROWS, HEAD), BF16),
            pltpu.VMEM((COLS, HEAD + SUMROWS, HEAD), BF16),
            pltpu.VMEM((COLS, HEAD + SUMROWS, HEAD), BF16),
            pltpu.VMEM((COLS, HEAD + SUMROWS, HEAD), BF16),
            pltpu.SMEM((GROUPS, 8, HEAD), jnp.int32),
            dma((COLS, GROUPS)), dma((COLS, GROUPS)), dma((COLS + 3,)),
            dma((GROUPS,)), dma((GROUPS,)), dma((GROUPS,)),
            dma((COLS,)), dma((COLS,)),
            dma((4, COLS)), dma((4, COLS)), dma((4, COLS)), dma((4, COLS)),
            dma((COLS,)), dma((COLS,)),
            dma((4, COLS)), dma((4, COLS)), dma((4, COLS)), dma((4, COLS)),
            dma((COLS,)), dma((COLS,)),
        ],
        compiler_params=pltpu.CompilerParams(
            collective_id=0, has_side_effects=True, vmem_limit_bytes=60 * 1024 * 1024
        ),
        name="spanned",
    )(
        page_owner.reshape(1, PAGES), page_slot, jnp.asarray(frequency), query_raw[0],
        suffix_keyval[0], query_gain[None], key_norm_gain[None], prefix_length, cache_pool[0],
    )
    return result.astype(BF16)[None]


def solution(mesh):
    finer = Mesh(mesh.devices.reshape(GROUPS, ROWS, COLS), ("group", "ctx_0", "ctx_1"))
    ctx = ("ctx_0", "ctx_1")
    in_specs = (
        P("group", ctx, None),
        P("group", ctx, None),
        P(),
        P(),
        P("group", ctx),
        P("group"),
        P("group", ctx, None),
        P("group", ctx),
        P("group", ctx, None, None),
    )
    return jax.shard_map(
        shards, mesh=finer, in_specs=in_specs, out_specs=P("group", ctx, None), check_vma=False
    )
```
